256 devices in a mesh: hist: 64 (over z, y, core), rep: 4 (over x).
Axes of the slice: x: 4, y: 4, z: 8, core: 2. Of those that a mesh axis runs over, the one named last changes fastest.
Arguments:
- features: bfloat16 [4, 16384, 512], P('rep', 'hist'), may hold values from -16 to 16
- history: bfloat16 [4, 131072, 512], P('rep', 'hist'), may hold values from -6 to 6
- blk_owner: int32 [4, 1024, 1], P('rep', 'hist'), may hold values from 0 to 63; in each aligned block of 16 rows (0 to 15, 16 to 31, ..., all dimensions but the last counted through in order) at most 2 rows name the same one
- blk_offset: int32 [4, 1024], P('rep', 'hist'), may hold values from 0 to 15
- blk_relation: int32 [4, 1024], P('rep', 'hist'), may hold values from 0 to 7
- adjacency: bfloat16 [4, 1024, 128, 128], P('rep', 'hist'), may hold values from -0.5 to 0.5
- weights: bfloat16 [9, 512, 512], replicated, may hold values from -0.09375 to 0.09375
- cotangent: bfloat16 [4, 16384, 512], P('rep', 'hist'), may hold values from -6 to 6
Outputs:
- fresh: bfloat16 [4, 16384, 512], P('rep', 'hist')
- grad_features: bfloat16 [4, 16384, 512], P('rep', 'hist')
- grad_weights: float32 [9, 262144], P(None, 'hist')
The draws below stay inside these ranges and needn't reach their ends.
Inputs may be any that keep to these rules, and one draw needn't show every extreme that they name: `blk_owner`: within the 16 rows of one device at most 2 blocks name one owner, and in every draw some owner is named by exactly 2 rows of some device.
All inputs are finite; a program needn't handle non-finite values.
Results may differ from the reference program's by a relative error of at most 0.0053.
Values may be sent and summed in bfloat16 or wider, within the bound.
A program may use at most 128 MiB of HBM per device.

```python
import math
import jax
import jax.numpy as jnp
import numpy as np
from jax import lax

D = 512
R = 8
TILE = 128
KB = 8
HT_DEV = 16
BT_DEV = 2
NBLK = 16
CAP = 2
BROWS = 256
HROWS = 2048
N_HIST = 64
N_REP = 4


def place_ends(drawn, key, least, top_value):
    shape = drawn.shape
    spot = [jax.random.randint(jax.random.fold_in(key, axis), (), 0, shape[axis]) for axis in range(len(shape))]
    drawn = drawn.at[tuple(spot)].set(least)
    longest = shape.index(max(shape))
    spot[longest] = (spot[longest] + 1) % shape[longest]
    return drawn.at[tuple(spot)].set(top_value)


def raised(array, key, source, target, blocks, factor):
    def block_of(position):
        return (jnp.arange(array.shape[position]) // (array.shape[position] // blocks)).reshape((-1,) + (1,) * (array.ndim - 1 - position))

    first = jax.random.permutation(key, blocks)[block_of(target)]
    second = (block_of(target) + blocks // 2) % blocks
    return jnp.where((block_of(source) == first) | (block_of(source) == second), factor * array, array)


def shard_levels(stream_key, extent, shards, low, largest):
    def one(position, blocks):
        steps = jax.random.uniform(jax.random.fold_in(jax.random.fold_in(stream_key, 6), position), (blocks,), jnp.float32, low / len(shards), largest / len(shards))
        return jnp.repeat(jnp.exp(steps), extent[position] // blocks).reshape((-1,) + (1,) * (len(extent) - position - 1))

    factor_of = one(*shards[0])
    for cut in shards[1:]:
        factor_of = factor_of * one(*cut)
    return factor_of


def routed_block(own_key, own, number, rows, count, top, bound, skew):
    ranking = jax.random.permutation(own_key, count)
    packed, usual = shares(count, rows * top, bound, skew, True), shares(count, rows * top, bound, skew, False)
    places = jnp.arange(count)

    def named(tallies, rotation):
        used = int((tallies > 0).sum())
        fixed = max(1, used // 4)
        passed = fixed + (places - fixed + rotation * (used - fixed)) % max(1, count - fixed)
        return jnp.zeros((count,), jnp.int32).at[ranking[jnp.where(places < fixed, places, passed)]].set(jnp.asarray(tallies, jnp.int32))

    tallies = jnp.where(number % 4 == 0, named(packed, number // 4), named(usual, number - number // 4 - 1))
    mixed = jax.random.permutation(jax.random.fold_in(own, 3), count)
    donor, sink = mixed[0:count // 2 * 2:2], mixed[1:count // 2 * 2:2]
    room = jnp.minimum(tallies[donor] - 1, bound - tallies[sink]) // 2
    room = jnp.where((donor == ranking[0]) | (sink == ranking[0]) | (tallies[sink] == 0), 0, jnp.maximum(room, 0))
    passed = jax.random.randint(jax.random.fold_in(own, 4), (count // 2,), 0, 1 << 20) % (room + 1)
    tallies = tallies.at[donor].add(-passed).at[sink].add(passed)
    labels = jnp.searchsorted(jnp.cumsum(tallies), jnp.arange(rows * top), side="right").astype(jnp.int32)
    grid = labels.reshape(top, rows).T
    grid = grid[jax.random.permutation(jax.random.fold_in(own, 1), rows)]
    rotation = jax.random.randint(jax.random.fold_in(own, 2), (rows, 1), 0, top)
    return jnp.take_along_axis(grid, (jnp.arange(top)[None, :] + rotation) % top, axis=1)


def shares(count, total, limit, skew, full):
    loads = [(1 << 20) // math.isqrt(rank ** skew) + 1 for rank in range(1, count + 1)]
    largest = limit if full else min(limit, max(-(-total // count), total * loads[0] // sum(loads)))
    least = 1 if total - largest >= count - 1 else 0
    holding, rest = [largest] + [least] * (count - 1), total - largest - least * (count - 1)
    while rest > 0:
        free = [i for i in range(1, count) if holding[i] < largest] or [i for i in range(1, count) if holding[i] < limit]
        whole, left = sum([loads[i] for i in free]), rest
        for i in free:
            more = min(limit - holding[i], max(1, left * loads[i] // whole), rest)
            holding[i] = holding[i] + more
            rest = rest - more
    return np.array(holding)


def scatter_about(key, dims, deviation, bound, cuts=(), kind=jnp.bfloat16):
    entries = deviation * jax.random.normal(key, dims, jnp.float32)
    if cuts:
        entries = entries * shard_levels(key, dims, cuts, -0.22, 0.18)
    return jnp.clip(entries, -bound, bound).astype(kind)


def gaussian_with(own_key, shape, scale, limit, shards, heavy, kind=jnp.bfloat16):
    values = scale * jax.random.normal(own_key, shape, jnp.float32)
    if shards:
        values = values * shard_levels(own_key, shape, shards, -0.22, 0.18)
    return jnp.clip(raised(values, jax.random.fold_in(own_key, 3), *heavy), -limit, limit).astype(kind)


def setup_inputs(seed: int = 0) -> dict:
    keys = jax.random.split(jax.random.key(seed), 9)
    features = gaussian_with(keys[0], (N_REP, N_HIST * BROWS, D), 1.0, 16.0, ((0, 4), (1, 64)), (1, 2, 64, 4.0))
    history = scatter_about(keys[1], (N_REP, N_HIST * HROWS, D), 1.0, 6.0, ((0, 4), (1, 64)))
    blk_owner_keys = jax.random.split(jax.random.fold_in(keys[2], 1), N_REP * (N_HIST * NBLK) // NBLK)
    blk_owner_turns = jax.random.permutation(jax.random.fold_in(keys[2], 3), N_REP * (N_HIST * NBLK) // NBLK)
    blk_owner = jax.vmap(lambda own, number: routed_block(jax.random.fold_in(keys[2], 2), own, number, NBLK, N_HIST, 1, CAP, 2))(blk_owner_keys, blk_owner_turns).reshape((N_REP, N_HIST * NBLK, 1))
    blk_offset = place_ends(jax.random.randint(keys[3], (N_REP, N_HIST * NBLK), 0, HT_DEV), jax.random.fold_in(keys[3], 1), 0, HT_DEV - 1).astype(jnp.int32)
    blk_relation = place_ends(jax.random.randint(keys[4], (N_REP, N_HIST * NBLK), 0, R), jax.random.fold_in(keys[4], 1), 0, R - 1).astype(jnp.int32)
    adjacency = scatter_about(keys[5], (N_REP, N_HIST * NBLK, TILE, TILE), TILE ** -0.5, 0.5, ((0, 4), (1, 64)))
    weights = scatter_about(keys[6], (R + 1, D, D), (D * (R + 1)) ** -0.5, 0.09375)
    cotangent = scatter_about(keys[7], (N_REP, N_HIST * BROWS, D), 1.0, 6.0, ((0, 4), (1, 64)))
    return dict(features=features, history=history, blk_owner=blk_owner, blk_offset=blk_offset, blk_relation=blk_relation, adjacency=adjacency, weights=weights, cotangent=cotangent)


def reference(features, history, blk_owner, blk_offset, blk_relation, adjacency, weights, cotangent):
    devices_all = N_REP * N_HIST
    table = history.reshape(N_REP, N_HIST, HT_DEV, TILE, D)
    items = (
        jnp.arange(devices_all, dtype=jnp.int32),
        features.reshape(devices_all, BT_DEV, TILE, D),
        cotangent.reshape(devices_all, BT_DEV, TILE, D),
        blk_owner.reshape(devices_all, NBLK).astype(jnp.int32),
        blk_offset.reshape(devices_all, NBLK).astype(jnp.int32),
        blk_relation.reshape(devices_all, NBLK).astype(jnp.int32),
        adjacency.reshape(devices_all, NBLK, TILE, TILE),
    )
    weights_wide = weights.astype(jnp.float32)

    def one_device(total, item):
        device, local_x, local_g, owners, offsets, relation, tiles = item
        replica = device // N_HIST
        pulled = table[replica][owners, offsets]
        block_sum = jnp.einsum("bij,bjd->bid", tiles.astype(jnp.float32), pulled.astype(jnp.float32))
        block_sum = block_sum.reshape(BT_DEV, KB, TILE, D)
        onehot = (relation.reshape(BT_DEV, KB)[:, :, None] == jnp.arange(R, dtype=jnp.int32)[None, None, :]).astype(jnp.float32)
        mixed = jnp.einsum("tkr,tkid->trid", onehot, block_sum, precision=lax.Precision.HIGHEST).astype(jnp.bfloat16)
        stacked = jnp.concatenate([local_x[:, None], mixed], axis=1).astype(jnp.float32)
        pre = jnp.einsum("trid,rde->tie", stacked, weights_wide)
        sigma = jax.nn.sigmoid(pre)
        fresh = (local_x.astype(jnp.float32) + pre * sigma).astype(jnp.bfloat16)
        dpre = (local_g.astype(jnp.float32) * sigma * (1.0 + pre * (1.0 - sigma))).astype(jnp.bfloat16).astype(jnp.float32)
        grad_x = (local_g.astype(jnp.float32) + jnp.einsum("tie,de->tid", dpre, weights_wide[0])).astype(jnp.bfloat16)
        grad_w = jnp.einsum("trid,tie->rde", stacked, dpre)
        return total + grad_w, (fresh, grad_x)

    start = jnp.zeros((R + 1, D, D), jnp.float32)
    total, (fresh, grad_x) = lax.scan(one_device, start, items)
    fresh = fresh.reshape(N_REP, N_HIST * BROWS, D)
    grad_x = grad_x.reshape(N_REP, N_HIST * BROWS, D)
    return fresh, grad_x, total.reshape(R + 1, D * D)
```

```python
import functools

import jax
import jax.numpy as jnp
from jax import lax
from jax.experimental import pallas as pl
from jax.experimental.pallas import tpu as pltpu
from jax.sharding import PartitionSpec as P

Y = 4
CORES = 2
PLANE = Y * CORES
CHUNKS = 4


def place(plane_count):
    me = lax.axis_index("hist")
    z, y, c = me // PLANE, (me // CORES) % Y, me % CORES

    def hist(dz=0, dy=0, dc=0):
        zz = lax.rem(z + dz + plane_count, plane_count)
        yy = lax.rem(y + dy + Y, Y)
        cc = lax.rem(c + dc, CORES)
        return (zz * Y + yy) * CORES + cc

    return me, z, y, c, hist


def remote(src, dst, send, recv, **device):
    return pltpu.make_async_remote_copy(
        src_ref=src,
        dst_ref=dst,
        send_sem=send,
        recv_sem=recv,
        device_id=device,
        device_id_type=pl.DeviceIdType.MESH,
    )


def greet(partners):
    barrier = pltpu.get_barrier_semaphore()
    for device in partners:
        pl.semaphore_signal(
            barrier, inc=1, device_id=device, device_id_type=pl.DeviceIdType.MESH
        )
    pl.semaphore_wait(barrier, len(partners))


def gather_kernel(
    planes, table_ref, code_ref, out_ref,
    tabs, stage_far, stage_near, far, near, codes, code_words,
    load_sem, ring_send, ring_recv, far_send, far_recv, near_send, near_recv,
    code_send, code_recv, word_sem,
):
    me, z, y, c, hist = place(planes)
    sign = 1 - 2 * c
    half = planes // 2
    tiles = table_ref.shape[0]
    rows = table_ref.shape[2]
    slots = out_ref.shape[0]

    def part(chunk, rel, core, lo=0, n=tiles):
        return tabs[chunk].at[pl.ds((rel * CORES + core) * tiles + lo, n)]

    loads = [
        pltpu.make_async_copy(table_ref.at[:, r], part(r, 0, 0), load_sem.at[r])
        for r in range(CHUNKS)
    ]
    for copy in loads:
        copy.start()

    column = [hist(dz=sign * d) for d in range(1, planes)]
    right, left, partner = hist(dy=1), hist(dy=-1), hist(dc=1)
    ahead, behind = hist(dz=sign), hist(dz=-sign)
    greet([{"hist": d} for d in column + [right, left, partner]])

    own_code = pltpu.make_async_copy(code_ref, codes.at[0], code_recv.at[0])
    own_code.start()
    asks = []
    for d in range(1, planes):
        copy = remote(
            code_ref, codes.at[d], code_send.at[d], code_recv.at[d], hist=column[d - 1]
        )
        copy.start()
        asks.append(copy)

    def ring(chunk, which, src, dst, device):
        return remote(
            src, dst, ring_send.at[chunk, which], ring_recv.at[chunk, which], hist=device
        )

    h = tiles // 2
    moves = []
    for r in range(CHUNKS):
        moves.append([
            ring(r, 0, part(r, 0, 0), part(r, 1, 0), right),
            ring(r, 1, part(r, 0, 0), part(r, 2, 0), left),
            ring(r, 2, part(r, 0, 0), part(r, 0, 1), partner),
            ring(r, 3, part(r, 1, 0, 0, h), part(r, 3, 0, 0, h), right),
            ring(r, 4, part(r, 2, 0, h, h), part(r, 3, 0, h, h), left),
            ring(r, 5, part(r, 1, 0), part(r, 1, 1), partner),
            ring(r, 6, part(r, 2, 0), part(r, 2, 1), partner),
            ring(r, 7, part(r, 3, 0, 0, h), part(r, 3, 1, 0, h), partner),
            ring(r, 8, part(r, 3, 0, h, h), part(r, 3, 1, h, h), partner),
        ])

    def own_out(r):
        loads[r].wait()
        for m in (0, 1, 2):
            moves[r][m].start()

    def pass_on(r):
        moves[r][0].wait_recv()
        moves[r][3].start()
        moves[r][1].wait_recv()
        moves[r][4].start()
        moves[r][5].start()
        moves[r][6].start()

    def across(r):
        moves[r][3].wait_recv()
        moves[r][7].start()
        moves[r][4].wait_recv()
        moves[r][8].start()

    def plane_ready(r):
        for m in (2, 5, 6, 7, 8):
            moves[r][m].wait_recv()

    def fill(r, dst, slot, merge):
        def body(i, carry):
            code = code_words[slot, 0, i]
            tile = tabs[r][lax.rem(code, PLANE * tiles)]
            if merge:
                tile = jnp.where(code // (PLANE * tiles) == z, tile, dst[i])
            dst[i] = tile
            return carry

        lax.fori_loop(0, slots, body, 0)

    far_moves = [
        [
            remote(
                stage_far.at[r] if s == 0 else far.at[r, s - 1], far.at[r, s],
                far_send.at[r, s], far_recv.at[r, s], hist=ahead,
            )
            for s in range(half)
        ]
        for r in range(CHUNKS)
    ]
    near_moves = [
        [
            remote(
                stage_near.at[r] if s == 0 else near.at[r, s - 1], near.at[r, s],
                near_send.at[r, s], near_recv.at[r, s], hist=behind,
            )
            for s in range(half - 1)
        ]
        for r in range(CHUNKS)
    ]

    def step(r, s):
        distance = half - s
        if s == 0:
            fill(r, stage_far.at[r], planes - distance, False)
        else:
            far_moves[r][s - 1].wait_recv()
            fill(r, far.at[r, s - 1], planes - distance, True)
        far_moves[r][s].start()
        if s < half - 1:
            distance = half - 1 - s
            if s == 0:
                fill(r, stage_near.at[r], distance, False)
            else:
                near_moves[r][s - 1].wait_recv()
                fill(r, near.at[r, s - 1], distance, True)
            near_moves[r][s].start()

    def finish(r):
        near_moves[r][half - 2].wait_recv()
        far_moves[r][half - 1].wait_recv()

        def body(i, carry):
            code = code_words[0, 0, i]
            source = code // (PLANE * tiles)
            tile = tabs[r][lax.rem(code, PLANE * tiles)]
            away = lax.rem(sign * (z - source) + planes, planes)
            other = jnp.where(away <= half, far[r, half - 1, i], near[r, half - 2, i])
            out_ref[i, pl.ds(r * rows, rows)] = jnp.where(away == 0, tile, other)
            return carry

        lax.fori_loop(0, slots, body, 0)

    def words():
        own_code.wait()
        for copy in asks:
            copy.wait_recv()
        copy = pltpu.make_async_copy(codes, code_words, word_sem)
        copy.start()
        copy.wait()

    events = [(-9, own_out, (0,)), (-8, words, ()), (-7, pass_on, (0,))]
    for r in range(CHUNKS):
        if r:
            events.append((half * r - half + 0.5, pass_on, (r,)))
            events.append((half * r - half + 2.5, across, (r,)))
        else:
            events.append((-5, across, (r,)))
        if r + 1 < CHUNKS:
            events.append((half * (r - 1) + 0.6 if r else -6, own_out, (r + 1,)))
        events.append((half * r - 0.5, plane_ready, (r,)))
        for s in range(half):
            events.append((half * r + 2 * s + 0.01 * r, step, (r, s)))
        events.append((half * r + 2 * half + 0.7, finish, (r,)))
    for _, act, args in sorted(events, key=lambda e: e[0]):
        act(*args)

    for group in moves + far_moves + near_moves + [asks]:
        for copy in group:
            copy.wait_send()


def pull(planes, table, code):
    tiles, tile_rows, width = table.shape
    slots = tiles
    rows = tile_rows // CHUNKS
    half = planes // 2
    dma = pltpu.SemaphoreType.DMA
    block = (slots, rows, width)
    return pl.pallas_call(
        functools.partial(gather_kernel, planes),
        out_shape=jax.ShapeDtypeStruct((slots, tile_rows, width), table.dtype),
        in_specs=[
            pl.BlockSpec(memory_space=pl.ANY),
            pl.BlockSpec(memory_space=pltpu.VMEM),
        ],
        out_specs=pl.BlockSpec(memory_space=pltpu.VMEM),
        scratch_shapes=[
            [pltpu.VMEM((PLANE * tiles, rows, width), table.dtype)] * CHUNKS,
            pltpu.VMEM((CHUNKS,) + block, table.dtype),
            pltpu.VMEM((CHUNKS,) + block, table.dtype),
            pltpu.VMEM((CHUNKS, half) + block, table.dtype),
            pltpu.VMEM((CHUNKS, half - 1) + block, table.dtype),
            pltpu.VMEM((planes, 8, 128), jnp.int32),
            pltpu.SMEM((planes, 8, 128), jnp.int32),
            dma((CHUNKS,)),
            dma((CHUNKS, 9)),
            dma((CHUNKS, 9)),
            dma((CHUNKS, half)),
            dma((CHUNKS, half)),
            dma((CHUNKS, half - 1)),
            dma((CHUNKS, half - 1)),
            dma((planes,)),
            dma((planes,)),
            dma(()),
        ],
        compiler_params=pltpu.CompilerParams(
            collective_id=0, has_side_effects=True, vmem_limit_bytes=60 << 20
        ),
    )(table.reshape(tiles, CHUNKS, rows, width), code)


GROUPS = 3


def layer_kernel(
    planes, reps, relation_ref, pulled_ref, adjacency_ref, features_ref, cotangent_ref, weights_ref,
    fresh_ref, grad_x_ref, grad_w_ref,
    masked, stacked, pre_ref, dpre_ref, product, kept, give, take,
    to_right, to_left, opposite, half_in, from_left, from_right, mine, z_out, z_in, share,
    pair_send, pair_recv, y_send, y_recv, z_send, z_recv, x_send, x_recv,
):
    me, z, y, c, hist = place(planes)
    x = lax.axis_index("rep")
    blocks, tile, width = pulled_ref.shape
    mats = weights_ref.shape[0]
    relations = mats - 1
    batch_tiles = features_ref.shape[0] // tile
    per_tile = blocks // batch_tiles
    own_rows = width // (planes * PLANE)
    per = mats // GROUPS

    right, left, partner = hist(dy=1), hist(dy=-1), hist(dc=1)
    column = [hist(dz=d) for d in range(1, planes)]
    others = [lax.rem(x + d, reps) for d in range(1, reps)]
    greet(
        [{"hist": d} for d in column + [right, left, partner]] + [{"rep": d} for d in others]
    )

    stacked[0] = features_ref[...]

    def mix(i, carry):
        t, q = i // relations, lax.rem(i, relations)
        for k in range(per_tile):
            hit = relation_ref[0, t * per_tile + k] == q
            block = adjacency_ref[t * per_tile + k]
            masked[:, k * tile:(k + 1) * tile] = jnp.where(hit, block, jnp.zeros_like(block))
        rhs = pulled_ref[pl.ds(t * per_tile, per_tile)].reshape(per_tile * tile, width)
        total = jnp.dot(masked[...], rhs, preferred_element_type=jnp.float32)
        stacked[1 + q, pl.ds(t * tile, tile)] = total.astype(stacked.dtype)
        return carry

    lax.fori_loop(0, batch_tiles * relations, mix, 0)

    pre_ref[...] = jnp.dot(stacked[0], weights_ref[0], preferred_element_type=jnp.float32)

    def project(j, carry):
        pre_ref[...] += jnp.dot(stacked[j], weights_ref[j], preferred_element_type=jnp.float32)
        return carry

    lax.fori_loop(1, mats, project, 0)

    wide_x = features_ref[...].astype(jnp.float32)
    wide_g = cotangent_ref[...].astype(jnp.float32)
    pre = pre_ref[...]
    sigma = jax.nn.sigmoid(pre)
    fresh_ref[...] = (wide_x + pre * sigma).astype(fresh_ref.dtype)
    dpre_ref[...] = (wide_g * sigma * (1.0 + pre * (1.0 - sigma))).astype(dpre_ref.dtype)

    pair = [
        remote(
            give.at[g], take.at[g], pair_send.at[g], pair_recv.at[g], hist=partner
        )
        for g in range(GROUPS)
    ]
    hr = planes * own_rows // 2

    def products(g):
        def one(i, carry):
            value = lax.dot_general(
                stacked[g * per + i], dpre_ref[...], (((0,), (0,)), ((), ())),
                preferred_element_type=jnp.float32,
            )
            product[...] = value.reshape(planes, Y, CORES, own_rows, width)
            for yy in range(Y):
                kept[g, yy, i] = product[:, yy, c].reshape(planes * own_rows, width)
                give[g, yy, i] = product[:, yy, 1 - c].reshape(
                    planes * own_rows, width
                ).astype(give.dtype)
            return carry

        lax.fori_loop(0, per, one, 0)
        pair[g].start()

    top, low = pl.ds(0, hr), pl.ds(hr, hr)

    def turn(g, which, src, dst, device):
        return remote(src, dst, y_send.at[g, which], y_recv.at[g, which], hist=device)

    turns = [
        [
            turn(g, 0, opposite.at[g, :, top], half_in.at[g, :, top], right),
            turn(g, 1, opposite.at[g, :, low], half_in.at[g, :, low], left),
            turn(g, 2, to_right.at[g, :, low], from_left.at[g, :, low], right),
            turn(g, 3, to_left.at[g, :, top], from_right.at[g, :, top], left),
            turn(g, 4, to_right.at[g, :, top], from_left.at[g, :, top], right),
            turn(g, 5, to_left.at[g, :, low], from_right.at[g, :, low], left),
        ]
        for g in range(GROUPS)
    ]
    y_right, y_left, y_far = lax.rem(y + 1, Y), lax.rem(y + Y - 1, Y), lax.rem(y + 2, Y)

    def y_first(g):
        pair[g].wait_recv()
        kind = opposite.dtype

        def one(i, carry):
            opposite[g, i] = (kept[g, y_far, i] + take[g, y_far, i].astype(jnp.float32)).astype(kind)
            right_sum = kept[g, y_right, i] + take[g, y_right, i].astype(jnp.float32)
            left_sum = kept[g, y_left, i] + take[g, y_left, i].astype(jnp.float32)
            to_right[g, i, low] = right_sum[hr:].astype(kind)
            to_left[g, i, top] = left_sum[:hr].astype(kind)
            kept[g, y_right, i] = right_sum
            kept[g, y_left, i] = left_sum
            return carry

        lax.fori_loop(0, per, one, 0)
        for m in range(4):
            turns[g][m].start()

    def y_second(g):
        turns[g][0].wait_recv()
        turns[g][1].wait_recv()

        def one(i, carry):
            up = kept[g, y_right, i, top] + half_in[g, i, top].astype(jnp.float32)
            down = kept[g, y_left, i, low] + half_in[g, i, low].astype(jnp.float32)
            to_right[g, i, top] = up.astype(to_right.dtype)
            to_left[g, i, low] = down.astype(to_left.dtype)
            return carry

        lax.fori_loop(0, per, one, 0)
        turns[g][4].start()
        turns[g][5].start()

    def y_last(g):
        for m in (2, 3, 4, 5):
            turns[g][m].wait_recv()

        def one(i, carry):
            total = kept[g, y, i] + take[g, y, i].astype(jnp.float32)
            total = total + from_left[g, i].astype(jnp.float32)
            total = total + from_right[g, i].astype(jnp.float32)
            mine[:, g * per + i] = total.reshape(planes, own_rows, width)
            return carry

        lax.fori_loop(0, per, one, 0)

    products(0)
    grad_x_ref[...] = (
        wide_g
        + lax.dot_general(
            dpre_ref[...], weights_ref[0], (((1,), (1,)), ((), ())),
            preferred_element_type=jnp.float32,
        )
    ).astype(grad_x_ref.dtype)
    for g in range(1, GROUPS):
        products(g)
        y_first(g - 1)
        if g > 1:
            y_second(g - 2)
    y_first(GROUPS - 1)
    if GROUPS > 1:
        y_second(GROUPS - 2)
    y_second(GROUPS - 1)
    for g in range(GROUPS):
        y_last(g)

    z_rows = mats * own_rows

    def stage_z(p, carry):
        z_out[p, pl.ds(0, z_rows)] = mine[p].reshape(z_rows, width).astype(z_out.dtype)
        return carry

    lax.fori_loop(0, planes, stage_z, 0)
    z_moves = []
    for d in range(1, planes):
        to = lax.rem(z + d, planes)
        copy = remote(
            z_out.at[to], z_in.at[d], z_send.at[d], z_recv.at[d], hist=column[d - 1]
        )
        copy.start()
        z_moves.append(copy)
    total = mine[z].reshape(z_rows, width)
    for d in range(1, planes):
        z_moves[d - 1].wait_recv()
        total = total + z_in[d, pl.ds(0, z_rows)].astype(jnp.float32)

    share[x] = total
    x_moves = []
    for d in range(1, reps):
        copy = remote(
            share.at[x], share.at[x], x_send.at[d], x_recv.at[d], rep=others[d - 1]
        )
        copy.start()
        x_moves.append(copy)
    for copy in x_moves:
        copy.wait_recv()
    total = share[0]
    for d in range(1, reps):
        total = total + share[d]
    grad_w_ref[...] = total.reshape(grad_w_ref.shape)

    for group in [pair, z_moves, x_moves] + turns:
        for copy in group:
            copy.wait_send()


def layer(planes, reps, relation, pulled, tiles, features, cotangent, weights):
    mats, width, _ = weights.shape
    batch = features.shape[0]
    blocks, tile, _ = pulled.shape
    per_tile = blocks * tile // batch
    own_rows = width // (planes * PLANE)
    per = mats // GROUPS
    piece = planes * own_rows
    z_pad = -(-mats * own_rows // 16) * 16
    low, high = features.dtype, jnp.float32
    dma = pltpu.SemaphoreType.DMA
    vmem = pl.BlockSpec(memory_space=pltpu.VMEM)
    return pl.pallas_call(
        functools.partial(layer_kernel, planes, reps),
        out_shape=(
            jax.ShapeDtypeStruct((batch, width), low),
            jax.ShapeDtypeStruct((batch, width), low),
            jax.ShapeDtypeStruct((mats, own_rows, width), high),
        ),
        in_specs=[pl.BlockSpec(memory_space=pltpu.SMEM)] + [vmem] * 5,
        out_specs=(vmem, vmem, vmem),
        scratch_shapes=[
            pltpu.VMEM((tile, per_tile * tile), low),
            pltpu.VMEM((mats, batch, width), low),
            pltpu.VMEM((batch, width), high),
            pltpu.VMEM((batch, width), low),
            pltpu.VMEM((planes, Y, CORES, own_rows, width), high),
            pltpu.VMEM((GROUPS, Y, per, piece, width), high),
            pltpu.VMEM((GROUPS, Y, per, piece, width), low),
            pltpu.VMEM((GROUPS, Y, per, piece, width), low),
            pltpu.VMEM((GROUPS, per, piece, width), low),
            pltpu.VMEM((GROUPS, per, piece, width), low),
            pltpu.VMEM((GROUPS, per, piece, width), low),
            pltpu.VMEM((GROUPS, per, piece, width), low),
            pltpu.VMEM((GROUPS, per, piece, width), low),
            pltpu.VMEM((GROUPS, per, piece, width), low),
            pltpu.VMEM((planes, mats, own_rows, width), high),
            pltpu.VMEM((planes, z_pad, width), low),
            pltpu.VMEM((planes, z_pad, width), low),
            pltpu.VMEM((reps, mats * own_rows, width), high),
            dma((GROUPS,)),
            dma((GROUPS,)),
            dma((GROUPS, 6)),
            dma((GROUPS, 6)),
            dma((planes,)),
            dma((planes,)),
            dma((reps,)),
            dma((reps,)),
        ],
        compiler_params=pltpu.CompilerParams(
            collective_id=1, has_side_effects=True, vmem_limit_bytes=60 << 20
        ),
    )(relation, pulled, tiles, features, cotangent, weights)


def on_device(
    planes, reps, features, history, blk_owner, blk_offset, blk_relation, adjacency, weights, cotangent
):
    owners = blk_owner.reshape(1, -1)
    tiles = adjacency[0]
    tile_rows = tiles.shape[-1]
    width = weights.shape[-1]
    mats = weights.shape[0]
    table = history.reshape(-1, tile_rows, width)

    me = lax.axis_index("hist")
    y, c = (me // CORES) % Y, me % CORES
    away = ((owners // CORES) % Y - y + Y) % Y
    rel = jnp.where(away == 0, 0, jnp.where(away == 3, 1, jnp.where(away == 1, 2, 3)))
    core = jnp.abs(owners % CORES - c)
    spot = (rel * CORES + core) * table.shape[0] + blk_offset.reshape(1, -1)
    code = (owners // PLANE) * (PLANE * table.shape[0]) + spot
    code = jnp.pad(code, ((0, 7), (0, 128 - code.shape[1])))

    pulled = pull(planes, table, code)
    fresh, grad_x, grad_w = layer(
        planes, reps, blk_relation, pulled, tiles, features[0], cotangent[0], weights
    )
    return fresh[None], grad_x[None], grad_w.reshape(mats, -1)


def solution(mesh):
    planes = mesh.shape["hist"] // PLANE
    in_specs = (
        P("rep", "hist", None),
        P("rep", "hist", None),
        P("rep", "hist", None),
        P("rep", "hist"),
        P("rep", "hist"),
        P("rep", "hist", None, None),
        P(),
        P("rep", "hist", None),
    )
    out_specs = (P("rep", "hist", None), P("rep", "hist", None), P(None, "hist"))
    return jax.shard_map(
        functools.partial(on_device, planes, mesh.shape["rep"]),
        mesh=mesh, in_specs=in_specs, out_specs=out_specs, check_vma=False,
    )
```

```python
import functools

import jax
import jax.numpy as jnp
from jax import lax
from jax.experimental import pallas as pl
from jax.experimental.pallas import tpu as pltpu
from jax.sharding import PartitionSpec as P

Y = 4
CORES = 2
PLANE = Y * CORES
CHUNKS = 4


def position(index):
    return lax.div(index, PLANE), lax.rem(lax.div(index, CORES), Y), lax.rem(index, CORES)


def place(plane_count):
    me = lax.axis_index("hist")
    z, y, c = position(me)

    def hist(dz=0, dy=0, dc=0):
        zz = lax.rem(z + dz + plane_count, plane_count)
        yy = lax.rem(y + dy + Y, Y)
        cc = lax.rem(c + dc, CORES)
        return (zz * Y + yy) * CORES + cc

    return me, z, y, c, hist


def remote(src, dst, send, recv, **device):
    return pltpu.make_async_remote_copy(
        src_ref=src,
        dst_ref=dst,
        send_sem=send,
        recv_sem=recv,
        device_id=device,
        device_id_type=pl.DeviceIdType.MESH,
    )


def greet(partners):
    barrier = pltpu.get_barrier_semaphore()
    for device in partners:
        pl.semaphore_signal(
            barrier, inc=1, device_id=device, device_id_type=pl.DeviceIdType.MESH
        )
    pl.semaphore_wait(barrier, len(partners))


def plane_moves(part, link, tiles, right, left, partner):
    h = tiles // 2
    return [
        link(0, part(0, 0), part(1, 0), right),
        link(1, part(0, 0), part(2, 0), left),
        link(2, part(0, 0), part(0, 1), partner),
        link(3, part(1, 0, 0, h), part(3, 0, 0, h), right),
        link(4, part(2, 0, h, h), part(3, 0, h, h), left),
        link(5, part(1, 0), part(1, 1), partner),
        link(6, part(2, 0), part(2, 1), partner),
        link(7, part(3, 0, 0, h), part(3, 1, 0, h), partner),
        link(8, part(3, 0, h, h), part(3, 1, h, h), partner),
    ]


def own_out(moves):
    for m in (0, 1, 2):
        moves[m].start()


def pass_on(moves):
    moves[0].wait_recv()
    moves[3].start()
    moves[1].wait_recv()
    moves[4].start()
    moves[5].start()
    moves[6].start()


def across(moves):
    moves[3].wait_recv()
    moves[7].start()
    moves[4].wait_recv()
    moves[8].start()


def plane_ready(moves):
    for m in (2, 5, 6, 7, 8):
        moves[m].wait_recv()


def part_of(ref, tiles):
    def part(rel, core, lo=0, n=tiles):
        return ref.at[pl.ds((rel * CORES + core) * tiles + lo, n)]

    return part


def ask_kernel(
    planes, reps, table_ref, code_ref, tab_ref, codes, level_ref,
    flags, plane_flags, rep_flags, own_sem, load_sem, code_send, code_recv,
    flag_send, flag_recv, top_send, top_recv, ring_send, ring_recv,
):
    me, z, y, c, hist = place(planes)
    sign = 1 - 2 * c
    x = lax.axis_index("rep")
    tiles = table_ref.shape[0]
    part = part_of(tab_ref, tiles)
    load = pltpu.make_async_copy(table_ref.at[:, 0], part(0, 0), load_sem)
    load.start()
    right, left, partner = hist(dy=1), hist(dy=-1), hist(dc=1)
    column = [hist(dz=sign * d) for d in range(1, planes)]
    plane = [hist(dy=d // CORES, dc=d % CORES) for d in range(1, PLANE)]
    others = [lax.rem(x + d, reps) for d in range(1, reps)]
    greet(
        [{"hist": d} for d in column + plane] + [{"rep": d} for d in others]
    )

    own = pltpu.make_async_copy(code_ref, codes.at[0], own_sem)
    own.start()
    asks = []
    for d in range(1, planes):
        copy = remote(
            code_ref, codes.at[d], code_send.at[d], code_recv.at[d], hist=column[d - 1]
        )
        copy.start()
        asks.append(copy)

    def link(which, src, dst, device):
        return remote(src, dst, ring_send.at[which], ring_recv.at[which], hist=device)

    moves = plane_moves(part, link, tiles, right, left, partner)
    load.wait()
    own_out(moves)

    own.wait()
    for copy in asks:
        copy.wait_recv()
    top = codes[0]
    for d in range(1, planes):
        top = jnp.maximum(top, codes[d])
    flags[0] = top
    spread = []
    for d in range(1, PLANE):
        copy = remote(
            flags.at[0], plane_flags.at[d], flag_send.at[d], flag_recv.at[d], hist=plane[d - 1]
        )
        copy.start()
        spread.append(copy)
    for d in range(1, PLANE):
        spread[d - 1].wait_recv()
        top = jnp.maximum(top, plane_flags[d])
    flags[1] = top
    over = []
    for d in range(1, reps):
        copy = remote(
            flags.at[1], rep_flags.at[d], top_send.at[d], top_recv.at[d], rep=others[d - 1]
        )
        copy.start()
        over.append(copy)
    for d in range(1, reps):
        over[d - 1].wait_recv()
        top = jnp.maximum(top, rep_flags[d])
    level_ref[...] = top

    pass_on(moves)
    across(moves)
    plane_ready(moves)
    for group in (asks, spread, over, moves):
        for copy in group:
            copy.wait_send()


def ask(planes, reps, table, code):
    tiles, chunks, rows, width = table.shape
    dma = pltpu.SemaphoreType.DMA
    vmem = pl.BlockSpec(memory_space=pltpu.VMEM)
    words = pltpu.VMEM
    return pl.pallas_call(
        functools.partial(ask_kernel, planes, reps),
        out_shape=(
            jax.ShapeDtypeStruct((PLANE * tiles, rows, width), table.dtype),
            jax.ShapeDtypeStruct((planes, 8, 128), jnp.int32),
            jax.ShapeDtypeStruct((8, 128), jnp.int32),
        ),
        in_specs=[pl.BlockSpec(memory_space=pl.ANY), vmem],
        out_specs=(vmem, vmem, vmem),
        scratch_shapes=[
            words((2, 8, 128), jnp.int32),
            words((PLANE, 8, 128), jnp.int32),
            words((reps, 8, 128), jnp.int32),
            dma(()),
            dma(()),
            dma((planes,)),
            dma((planes,)),
            dma((PLANE,)),
            dma((PLANE,)),
            dma((reps,)),
            dma((reps,)),
            dma((9,)),
            dma((9,)),
        ],
        compiler_params=pltpu.CompilerParams(collective_id=0, has_side_effects=True),
    )(table, code)


def gather_kernel(
    planes, far_room, near_room, table_ref, first_ref, codes, out_ref,
    tabs, stage_far, stage_near, far, near, far_end, near_end,
    load_sem, ring_send, ring_recv, far_send, far_recv, near_send, near_recv,
):
    me, z, y, c, hist = place(planes)
    sign = 1 - 2 * c
    half = planes // 2
    tiles = table_ref.shape[0]
    rows = table_ref.shape[2]
    slots = out_ref.shape[0]

    loads = [pltpu.make_async_copy(first_ref, tabs[0], load_sem.at[0])] + [
        pltpu.make_async_copy(
            table_ref.at[:, r], tabs[r].at[pl.ds(0, tiles)], load_sem.at[r]
        )
        for r in range(1, CHUNKS)
    ]
    for copy in loads:
        copy.start()

    right, left, partner = hist(dy=1), hist(dy=-1), hist(dc=1)
    ahead, behind = hist(dz=sign), hist(dz=-sign)
    greet([{"hist": d} for d in (right, left, partner, ahead, behind)])

    moves = [[]]
    for r in range(1, CHUNKS):
        def link(which, src, dst, device, r=r):
            return remote(
                src, dst, ring_send.at[r, which], ring_recv.at[r, which], hist=device
            )

        moves.append(plane_moves(part_of(tabs[r], tiles), link, tiles, right, left, partner))

    def begin(r):
        loads[r].wait()
        own_out(moves[r])

    def fill(r, dst, slot, lane, count, merge):
        def body(i, carry):
            code = codes[slot, lane, i]
            tile = tabs[r][lax.rem(code, PLANE * tiles)]
            if merge:
                tile = jnp.where(lax.div(code, PLANE * tiles) == z, tile, dst[i])
            dst[i] = tile
            return carry

        lax.fori_loop(0, count, body, 0, unroll=2)

    def chain(stage, middle, end, room, send, recv, device):
        last = len(room) - 1
        ready = []
        for r in range(CHUNKS):
            hops = []
            for s, count in enumerate(room):
                src = stage.at[r] if s == 0 else middle.at[r, s - 1]
                dst = end[r] if s == last else middle.at[r, s]
                some = pl.ds(0, count)
                hops.append(
                    remote(src.at[some], dst.at[some], send.at[r, s], recv.at[r, s], hist=device)
                )
            ready.append(hops)
        return ready

    far_moves = chain(stage_far, far, far_end, far_room, far_send, far_recv, ahead)
    near_moves = chain(stage_near, near, near_end, near_room, near_send, near_recv, behind)

    def step(r, s):
        if s == 0:
            fill(r, stage_far.at[r], planes - half, 0, far_room[0], False)
        else:
            far_moves[r][s - 1].wait_recv()
            fill(r, far.at[r, s - 1], planes - half + s, 0, far_room[s], True)
        far_moves[r][s].start()
        if s < half - 1:
            distance = half - 1 - s
            if s == 0:
                fill(r, stage_near.at[r], distance, 1, near_room[0], False)
            else:
                near_moves[r][s - 1].wait_recv()
                fill(r, near.at[r, s - 1], distance, 1, near_room[s], True)
            near_moves[r][s].start()

    def finish(r):
        near_moves[r][half - 2].wait_recv()
        far_moves[r][half - 1].wait_recv()

        def body(i, carry):
            kind = codes[0, 2, i]
            spot = codes[0, 3, i]
            tile = tabs[r][codes[0, 4, i]]
            other = jnp.where(kind == 1, far_end[r][spot], near_end[r][spot])
            out_ref[i, pl.ds(r * rows, rows)] = jnp.where(kind == 0, tile, other)
            return carry

        lax.fori_loop(0, slots, body, 0, unroll=2)

    def first():
        loads[0].wait()

    events = [(-9, first, ())]
    for r in range(CHUNKS):
        if r:
            events.append((half * r - half + 0.5, pass_on, (moves[r],)))
            events.append((half * r - half + 2.5, across, (moves[r],)))
            events.append((half * r - 0.5, plane_ready, (moves[r],)))
        if r + 1 < CHUNKS:
            events.append((half * (r - 1) + 0.6 if r else -8, begin, (r + 1,)))
        for s in range(half):
            events.append((half * r + 2 * s + 0.01 * r, step, (r, s)))
        events.append((half * r + 2 * half + 0.7, finish, (r,)))
    for _, act, args in sorted(events, key=lambda e: e[0]):
        act(*args)

    for group in moves + far_moves + near_moves:
        for copy in group:
            copy.wait_send()


def pull(planes, level, far_room, near_room, table, first, codes):
    tiles, chunks, rows, width = table.shape
    slots = tiles
    half = planes // 2
    dma = pltpu.SemaphoreType.DMA
    block = (slots, rows, width)
    hbm = pl.BlockSpec(memory_space=pl.ANY)
    return pl.pallas_call(
        functools.partial(gather_kernel, planes, far_room, near_room),
        out_shape=jax.ShapeDtypeStruct((slots, chunks * rows, width), table.dtype),
        in_specs=[hbm, hbm, pl.BlockSpec(memory_space=pltpu.SMEM)],
        out_specs=pl.BlockSpec(memory_space=pltpu.VMEM),
        scratch_shapes=[
            [pltpu.VMEM((PLANE * tiles, rows, width), table.dtype)] * chunks,
            pltpu.VMEM((chunks,) + block, table.dtype),
            pltpu.VMEM((chunks,) + block, table.dtype),
            pltpu.VMEM((chunks, half - 1) + block, table.dtype),
            pltpu.VMEM((chunks, half - 2) + block, table.dtype),
            [pltpu.VMEM(block, table.dtype)] * chunks,
            [pltpu.VMEM(block, table.dtype)] * chunks,
            dma((chunks,)),
            dma((chunks, 9)),
            dma((chunks, 9)),
            dma((chunks, half)),
            dma((chunks, half)),
            dma((chunks, half - 1)),
            dma((chunks, half - 1)),
        ],
        compiler_params=pltpu.CompilerParams(
            collective_id=2 + level, has_side_effects=True, vmem_limit_bytes=60 << 20
        ),
    )(table, first, codes)


def rooms(planes, slots):
    half = planes // 2
    full = ((slots,) * half, (slots,) * (half - 1))
    if (planes, slots) != (8, 16):
        return [full]
    return [
        ((6, 9, 11, 13), (6, 9, 11)),
        ((8, 12, 14, 15), (8, 12, 14)),
        full,
    ]


def requests(planes, levels, tiles, owners, offsets):
    me = lax.axis_index("hist")
    z, y, c = position(me)
    oz, oy, oc = position(owners)
    half = planes // 2
    slots = owners.shape[0]
    sign = 1 - 2 * c
    turn = lax.rem(oy - y + Y, Y)
    rel = jnp.where(turn == 0, 0, jnp.where(turn == 3, 1, jnp.where(turn == 1, 2, 3)))
    tile = (rel * CORES + jnp.abs(oc - c)) * tiles + offsets
    code = oz * (PLANE * tiles) + tile
    away = lax.rem(sign * (z - oz) + planes, planes)
    place = jnp.arange(slots)
    far = (away >= 1) & (away <= half)
    near = away > half
    keys = jnp.stack([jnp.where(far, half - away, planes), jnp.where(near, away, 2 * planes)])
    keys = keys * slots + place
    rank = jnp.sum((keys[:, None, :] < keys[:, :, None]).astype(jnp.int32), axis=2)
    hit = rank[:, :, None] == place
    ordered = jnp.sum(jnp.where(hit, code[None, :, None], 0), axis=1)
    kind = jnp.where(far, 1, jnp.where(near, 2, 0))
    spot = jnp.where(far, rank[0], rank[1])
    level = jnp.int32(0)
    for far_room, near_room in levels[:-1]:
        over = jnp.bool_(False)
        for s, room in enumerate(far_room):
            over |= jnp.sum((far & (away >= half - s)).astype(jnp.int32)) > room
        for s, room in enumerate(near_room):
            over |= jnp.sum((near & (away <= half + 1 + s)).astype(jnp.int32)) > room
        level = level + over.astype(jnp.int32)
    words = jnp.concatenate(
        [ordered, jnp.stack([kind, spot, tile, jnp.broadcast_to(level, (slots,))])]
    )
    return jnp.pad(words, ((0, 2), (0, 128 - slots)))


GROUPS = 3


def layer_kernel(
    planes, reps, relation_ref, pulled_ref, adjacency_ref, features_ref, cotangent_ref, weights_ref,
    fresh_ref, grad_x_ref, grad_w_ref,
    masked, stacked, pre_ref, dpre_ref, product, kept, give, take,
    to_right, to_left, opposite, half_in, from_left, from_right, mine, z_out, z_in, share,
    pair_send, pair_recv, y_send, y_recv, z_send, z_recv, x_send, x_recv,
):
    me, z, y, c, hist = place(planes)
    x = lax.axis_index("rep")
    blocks, tile, width = pulled_ref.shape
    mats = weights_ref.shape[0]
    relations = mats - 1
    batch_tiles = features_ref.shape[0] // tile
    per_tile = blocks // batch_tiles
    own_rows = width // (planes * PLANE)
    per = mats // GROUPS

    right, left, partner = hist(dy=1), hist(dy=-1), hist(dc=1)
    column = [hist(dz=d) for d in range(1, planes)]
    others = [lax.rem(x + d, reps) for d in range(1, reps)]
    greet(
        [{"hist": d} for d in column + [right, left, partner]] + [{"rep": d} for d in others]
    )

    stacked[0] = features_ref[...]

    def mix(i, carry):
        t, q = lax.div(i, relations), lax.rem(i, relations)
        for k in range(per_tile):
            hit = relation_ref[0, t * per_tile + k] == q
            block = adjacency_ref[t * per_tile + k]
            masked[:, k * tile:(k + 1) * tile] = jnp.where(hit, block, jnp.zeros_like(block))
        rhs = pulled_ref[pl.ds(t * per_tile, per_tile)].reshape(per_tile * tile, width)
        total = jnp.dot(masked[...], rhs, preferred_element_type=jnp.float32)
        stacked[1 + q, pl.ds(t * tile, tile)] = total.astype(stacked.dtype)
        return carry

    lax.fori_loop(0, batch_tiles * relations, mix, 0)

    pre_ref[...] = jnp.dot(stacked[0], weights_ref[0], preferred_element_type=jnp.float32)

    def project(j, carry):
        pre_ref[...] += jnp.dot(stacked[j], weights_ref[j], preferred_element_type=jnp.float32)
        return carry

    lax.fori_loop(1, mats, project, 0)

    wide_x = features_ref[...].astype(jnp.float32)
    wide_g = cotangent_ref[...].astype(jnp.float32)
    pre = pre_ref[...]
    sigma = jax.nn.sigmoid(pre)
    fresh_ref[...] = (wide_x + pre * sigma).astype(fresh_ref.dtype)
    dpre_ref[...] = (wide_g * sigma * (1.0 + pre * (1.0 - sigma))).astype(dpre_ref.dtype)

    pair = [
        remote(
            give.at[g], take.at[g], pair_send.at[g], pair_recv.at[g], hist=partner
        )
        for g in range(GROUPS)
    ]
    hr = planes * own_rows // 2

    def products(g):
        def one(i, carry):
            value = lax.dot_general(
                stacked[g * per + i], dpre_ref[...], (((0,), (0,)), ((), ())),
                preferred_element_type=jnp.float32,
            )
            product[...] = value.reshape(planes, Y, CORES, own_rows, width)
            for yy in range(Y):
                kept[g, yy, i] = product[:, yy, c].reshape(planes * own_rows, width)
                give[g, yy, i] = product[:, yy, 1 - c].reshape(
                    planes * own_rows, width
                ).astype(give.dtype)
            return carry

        lax.fori_loop(0, per, one, 0)
        pair[g].start()

    top, low = pl.ds(0, hr), pl.ds(hr, hr)

    def turn(g, which, src, dst, device):
        return remote(src, dst, y_send.at[g, which], y_recv.at[g, which], hist=device)

    turns = [
        [
            turn(g, 0, opposite.at[g, :, top], half_in.at[g, :, top], right),
            turn(g, 1, opposite.at[g, :, low], half_in.at[g, :, low], left),
            turn(g, 2, to_right.at[g, :, low], from_left.at[g, :, low], right),
            turn(g, 3, to_left.at[g, :, top], from_right.at[g, :, top], left),
            turn(g, 4, to_right.at[g, :, top], from_left.at[g, :, top], right),
            turn(g, 5, to_left.at[g, :, low], from_right.at[g, :, low], left),
        ]
        for g in range(GROUPS)
    ]
    y_right, y_left, y_far = lax.rem(y + 1, Y), lax.rem(y + Y - 1, Y), lax.rem(y + 2, Y)

    def y_first(g):
        pair[g].wait_recv()
        kind = opposite.dtype

        def one(i, carry):
            opposite[g, i] = (kept[g, y_far, i] + take[g, y_far, i].astype(jnp.float32)).astype(kind)
            right_sum = kept[g, y_right, i] + take[g, y_right, i].astype(jnp.float32)
            left_sum = kept[g, y_left, i] + take[g, y_left, i].astype(jnp.float32)
            to_right[g, i, low] = right_sum[hr:].astype(kind)
            to_left[g, i, top] = left_sum[:hr].astype(kind)
            kept[g, y_right, i] = right_sum
            kept[g, y_left, i] = left_sum
            return carry

        lax.fori_loop(0, per, one, 0)
        for m in range(4):
            turns[g][m].start()

    def y_second(g):
        turns[g][0].wait_recv()
        turns[g][1].wait_recv()

        def one(i, carry):
            up = kept[g, y_right, i, top] + half_in[g, i, top].astype(jnp.float32)
            down = kept[g, y_left, i, low] + half_in[g, i, low].astype(jnp.float32)
            to_right[g, i, top] = up.astype(to_right.dtype)
            to_left[g, i, low] = down.astype(to_left.dtype)
            return carry

        lax.fori_loop(0, per, one, 0)
        turns[g][4].start()
        turns[g][5].start()

    def y_last(g):
        for m in (2, 3, 4, 5):
            turns[g][m].wait_recv()

        def one(i, carry):
            total = kept[g, y, i] + take[g, y, i].astype(jnp.float32)
            total = total + from_left[g, i].astype(jnp.float32)
            total = total + from_right[g, i].astype(jnp.float32)
            mine[:, g * per + i] = total.reshape(planes, own_rows, width)
            return carry

        lax.fori_loop(0, per, one, 0)

    products(0)
    grad_x_ref[...] = (
        wide_g
        + lax.dot_general(
            dpre_ref[...], weights_ref[0], (((1,), (1,)), ((), ())),
            preferred_element_type=jnp.float32,
        )
    ).astype(grad_x_ref.dtype)
    for g in range(1, GROUPS):
        products(g)
        y_first(g - 1)
        if g > 1:
            y_second(g - 2)
    y_first(GROUPS - 1)
    if GROUPS > 1:
        y_second(GROUPS - 2)
    y_second(GROUPS - 1)
    for g in range(GROUPS):
        y_last(g)

    z_rows = mats * own_rows

    def stage_z(p, carry):
        z_out[p, pl.ds(0, z_rows)] = mine[p].reshape(z_rows, width).astype(z_out.dtype)
        return carry

    lax.fori_loop(0, planes, stage_z, 0)
    z_moves = []
    for d in range(1, planes):
        to = lax.rem(z + d, planes)
        copy = remote(
            z_out.at[to], z_in.at[d], z_send.at[d], z_recv.at[d], hist=column[d - 1]
        )
        copy.start()
        z_moves.append(copy)
    total = mine[z].reshape(z_rows, width)
    for d in range(1, planes):
        z_moves[d - 1].wait_recv()
        total = total + z_in[d, pl.ds(0, z_rows)].astype(jnp.float32)

    share[x] = total
    x_moves = []
    for d in range(1, reps):
        copy = remote(
            share.at[x], share.at[x], x_send.at[d], x_recv.at[d], rep=others[d - 1]
        )
        copy.start()
        x_moves.append(copy)
    for copy in x_moves:
        copy.wait_recv()
    total = share[0]
    for d in range(1, reps):
        total = total + share[d]
    grad_w_ref[...] = total.reshape(grad_w_ref.shape)

    for group in [pair, z_moves, x_moves] + turns:
        for copy in group:
            copy.wait_send()


def layer(planes, reps, relation, pulled, tiles, features, cotangent, weights):
    mats, width, _ = weights.shape
    batch = features.shape[0]
    blocks, tile, _ = pulled.shape
    per_tile = blocks * tile // batch
    own_rows = width // (planes * PLANE)
    per = mats // GROUPS
    piece = planes * own_rows
    z_pad = -(-mats * own_rows // 16) * 16
    low, high = features.dtype, jnp.float32
    dma = pltpu.SemaphoreType.DMA
    vmem = pl.BlockSpec(memory_space=pltpu.VMEM)
    return pl.pallas_call(
        functools.partial(layer_kernel, planes, reps),
        out_shape=(
            jax.ShapeDtypeStruct((batch, width), low),
            jax.ShapeDtypeStruct((batch, width), low),
            jax.ShapeDtypeStruct((mats, own_rows, width), high),
        ),
        in_specs=[pl.BlockSpec(memory_space=pltpu.SMEM)] + [vmem] * 5,
        out_specs=(vmem, vmem, vmem),
        scratch_shapes=[
            pltpu.VMEM((tile, per_tile * tile), low),
            pltpu.VMEM((mats, batch, width), low),
            pltpu.VMEM((batch, width), high),
            pltpu.VMEM((batch, width), low),
            pltpu.VMEM((planes, Y, CORES, own_rows, width), high),
            pltpu.VMEM((GROUPS, Y, per, piece, width), high),
            pltpu.VMEM((GROUPS, Y, per, piece, width), low),
            pltpu.VMEM((GROUPS, Y, per, piece, width), low),
            pltpu.VMEM((GROUPS, per, piece, width), low),
            pltpu.VMEM((GROUPS, per, piece, width), low),
            pltpu.VMEM((GROUPS, per, piece, width), low),
            pltpu.VMEM((GROUPS, per, piece, width), low),
            pltpu.VMEM((GROUPS, per, piece, width), low),
            pltpu.VMEM((GROUPS, per, piece, width), low),
            pltpu.VMEM((planes, mats, own_rows, width), high),
            pltpu.VMEM((planes, z_pad, width), low),
            pltpu.VMEM((planes, z_pad, width), low),
            pltpu.VMEM((reps, mats * own_rows, width), high),
            dma((GROUPS,)),
            dma((GROUPS,)),
            dma((GROUPS, 6)),
            dma((GROUPS, 6)),
            dma((planes,)),
            dma((planes,)),
            dma((reps,)),
            dma((reps,)),
        ],
        compiler_params=pltpu.CompilerParams(
            collective_id=1, has_side_effects=True, vmem_limit_bytes=60 << 20
        ),
    )(relation, pulled, tiles, features, cotangent, weights)


def on_device(
    planes, reps, features, history, blk_owner, blk_offset, blk_relation, adjacency, weights, cotangent
):
    owners = blk_owner.reshape(-1)
    tiles = adjacency[0]
    tile_rows = tiles.shape[-1]
    width = weights.shape[-1]
    mats = weights.shape[0]
    table = history.reshape(-1, tile_rows, width)

    tiles_held = table.shape[0]
    table = table.reshape(tiles_held, CHUNKS, tile_rows // CHUNKS, width)
    levels = rooms(planes, owners.shape[0])
    words = requests(planes, levels, tiles_held, owners, blk_offset.reshape(-1))
    first, codes, top = ask(planes, reps, table, words)
    pulled = lax.switch(
        top[5, 0],
        [
            functools.partial(pull, planes, level, far_room, near_room)
            for level, (far_room, near_room) in enumerate(levels)
        ],
        table, first, codes,
    )
    fresh, grad_x, grad_w = layer(
        planes, reps, blk_relation, pulled, tiles, features[0], cotangent[0], weights
    )
    return fresh[None], grad_x[None], grad_w.reshape(mats, -1)


def solution(mesh):
    planes = mesh.shape["hist"] // PLANE
    in_specs = (
        P("rep", "hist", None),
        P("rep", "hist", None),
        P("rep", "hist", None),
        P("rep", "hist"),
        P("rep", "hist"),
        P("rep", "hist", None, None),
        P(),
        P("rep", "hist", None),
    )
    out_specs = (P("rep", "hist", None), P("rep", "hist", None), P(None, "hist"))
    return jax.shard_map(
        functools.partial(on_device, planes, mesh.shape["rep"]),
        mesh=mesh, in_specs=in_specs, out_specs=out_specs, check_vma=False,
    )
```

```python
import functools

import jax
import jax.numpy as jnp
from jax import lax
from jax.experimental import pallas as pl
from jax.experimental.pallas import tpu as pltpu
from jax.sharding import PartitionSpec as P

Y = 4
CORES = 2
PLANE = Y * CORES
CHUNKS = 8
STRIDE = 3


def position(index):
    return lax.div(index, PLANE), lax.rem(lax.div(index, CORES), Y), lax.rem(index, CORES)


def place(plane_count):
    me = lax.axis_index("hist")
    z, y, c = position(me)

    def hist(dz=0, dy=0, dc=0):
        zz = lax.rem(z + dz + plane_count, plane_count)
        yy = lax.rem(y + dy + Y, Y)
        cc = lax.rem(c + dc, CORES)
        return (zz * Y + yy) * CORES + cc

    return me, z, y, c, hist


def remote(src, dst, send, recv, **device):
    return pltpu.make_async_remote_copy(
        src_ref=src,
        dst_ref=dst,
        send_sem=send,
        recv_sem=recv,
        device_id=device,
        device_id_type=pl.DeviceIdType.MESH,
    )


def greet(partners):
    barrier = pltpu.get_barrier_semaphore()
    for device in partners:
        pl.semaphore_signal(
            barrier, inc=1, device_id=device, device_id_type=pl.DeviceIdType.MESH
        )
    pl.semaphore_wait(barrier, len(partners))


def plane_moves(part, link, tiles, right, left, partner):
    h = tiles // 2
    return [
        link(0, part(0, 0), part(1, 0), right),
        link(1, part(0, 0), part(2, 0), left),
        link(2, part(0, 0), part(0, 1), partner),
        link(3, part(1, 0, 0, h), part(3, 0, 0, h), right),
        link(4, part(2, 0, h, h), part(3, 0, h, h), left),
        link(5, part(1, 0), part(1, 1), partner),
        link(6, part(2, 0), part(2, 1), partner),
        link(7, part(3, 0, 0, h), part(3, 1, 0, h), partner),
        link(8, part(3, 0, h, h), part(3, 1, h, h), partner),
    ]


def own_out(moves):
    for m in (0, 1, 2):
        moves[m].start()


def pass_on(moves):
    moves[0].wait_recv()
    moves[3].start()
    moves[1].wait_recv()
    moves[4].start()
    moves[5].start()
    moves[6].start()


def across(moves):
    moves[3].wait_recv()
    moves[7].start()
    moves[4].wait_recv()
    moves[8].start()


def plane_ready(moves):
    for m in (2, 5, 6, 7, 8):
        moves[m].wait_recv()


def part_of(ref, tiles):
    def part(rel, core, lo=0, n=tiles):
        return ref.at[pl.ds((rel * CORES + core) * tiles + lo, n)]

    return part


def ask_kernel(
    planes, reps, table_ref, code_ref, tab_ref, codes, level_ref,
    flags, plane_flags, rep_flags, own_sem, load_sem, code_send, code_recv,
    flag_send, flag_recv, top_send, top_recv, ring_send, ring_recv,
):
    me, z, y, c, hist = place(planes)
    sign = 1 - 2 * c
    x = lax.axis_index("rep")
    tiles = table_ref.shape[0]
    part = part_of(tab_ref, tiles)
    load = pltpu.make_async_copy(table_ref.at[:, 0], part(0, 0), load_sem)
    load.start()
    right, left, partner = hist(dy=1), hist(dy=-1), hist(dc=1)
    column = [hist(dz=sign * d) for d in range(1, planes)]
    plane = [hist(dy=d // CORES, dc=d % CORES) for d in range(1, PLANE)]
    others = [lax.rem(x + d, reps) for d in range(1, reps)]
    greet(
        [{"hist": d} for d in column + plane] + [{"rep": d} for d in others]
    )

    own = pltpu.make_async_copy(code_ref, codes.at[0], own_sem)
    own.start()
    asks = []
    for d in range(1, planes):
        copy = remote(
            code_ref, codes.at[d], code_send.at[d], code_recv.at[d], hist=column[d - 1]
        )
        copy.start()
        asks.append(copy)

    def link(which, src, dst, device):
        return remote(src, dst, ring_send.at[which], ring_recv.at[which], hist=device)

    moves = plane_moves(part, link, tiles, right, left, partner)
    load.wait()
    own_out(moves)

    own.wait()
    for copy in asks:
        copy.wait_recv()
    top = codes[0]
    for d in range(1, planes):
        top = jnp.maximum(top, codes[d])
    flags[0] = top
    spread = []
    for d in range(1, PLANE):
        copy = remote(
            flags.at[0], plane_flags.at[d], flag_send.at[d], flag_recv.at[d], hist=plane[d - 1]
        )
        copy.start()
        spread.append(copy)
    pass_on(moves)
    for d in range(1, PLANE):
        spread[d - 1].wait_recv()
        top = jnp.maximum(top, plane_flags[d])
    flags[1] = top
    over = []
    for d in range(1, reps):
        copy = remote(
            flags.at[1], rep_flags.at[d], top_send.at[d], top_recv.at[d], rep=others[d - 1]
        )
        copy.start()
        over.append(copy)
    across(moves)
    for d in range(1, reps):
        over[d - 1].wait_recv()
        top = jnp.maximum(top, rep_flags[d])
    level_ref[...] = top

    plane_ready(moves)
    for group in (asks, spread, over, moves):
        for copy in group:
            copy.wait_send()


def ask(planes, reps, table, code):
    tiles, chunks, rows, width = table.shape
    dma = pltpu.SemaphoreType.DMA
    vmem = pl.BlockSpec(memory_space=pltpu.VMEM)
    words = pltpu.VMEM
    return pl.pallas_call(
        functools.partial(ask_kernel, planes, reps),
        out_shape=(
            jax.ShapeDtypeStruct((PLANE * tiles, rows, width), table.dtype),
            jax.ShapeDtypeStruct((planes, 8, 128), jnp.int32),
            jax.ShapeDtypeStruct((8, 128), jnp.int32),
        ),
        in_specs=[pl.BlockSpec(memory_space=pl.ANY), vmem],
        out_specs=(vmem, vmem, vmem),
        scratch_shapes=[
            words((2, 8, 128), jnp.int32),
            words((PLANE, 8, 128), jnp.int32),
            words((reps, 8, 128), jnp.int32),
            dma(()),
            dma(()),
            dma((planes,)),
            dma((planes,)),
            dma((PLANE,)),
            dma((PLANE,)),
            dma((reps,)),
            dma((reps,)),
            dma((9,)),
            dma((9,)),
        ],
        compiler_params=pltpu.CompilerParams(collective_id=0, has_side_effects=True),
    )(table, code)


def gather_kernel(
    planes, far_room, near_room, table_ref, first_ref, codes, out_ref,
    tabs, stage_far, stage_near, far, near, far_end, near_end,
    load_sem, ring_send, ring_recv, far_send, far_recv, near_send, near_recv,
):
    me, z, y, c, hist = place(planes)
    sign = 1 - 2 * c
    half = planes // 2
    tiles = table_ref.shape[0]
    rows = table_ref.shape[2]
    slots = out_ref.shape[0]

    loads = [pltpu.make_async_copy(first_ref, tabs[0], load_sem.at[0])] + [
        pltpu.make_async_copy(
            table_ref.at[:, r], tabs[r].at[pl.ds(0, tiles)], load_sem.at[r]
        )
        for r in range(1, CHUNKS)
    ]
    for copy in loads:
        copy.start()

    right, left, partner = hist(dy=1), hist(dy=-1), hist(dc=1)
    ahead, behind = hist(dz=sign), hist(dz=-sign)
    greet([{"hist": d} for d in (right, left, partner, ahead, behind)])

    moves = [[]]
    for r in range(1, CHUNKS):
        def link(which, src, dst, device, r=r):
            return remote(
                src, dst, ring_send.at[r, which], ring_recv.at[r, which], hist=device
            )

        moves.append(plane_moves(part_of(tabs[r], tiles), link, tiles, right, left, partner))

    def begin(r):
        loads[r].wait()
        own_out(moves[r])

    def fill(r, dst, slot, lane, count, merge):
        def body(i, carry):
            code = codes[slot, lane, i]
            tile = tabs[r][lax.rem(code, PLANE * tiles)]
            if merge:
                tile = jnp.where(lax.div(code, PLANE * tiles) == z, tile, dst[i])
            dst[i] = tile
            return carry

        lax.fori_loop(0, count, body, 0, unroll=2)

    def chain(stage, middle, end, room, send, recv, device):
        last = len(room) - 1
        ready = []
        for r in range(CHUNKS):
            hops = []
            for s, count in enumerate(room):
                src = stage.at[r] if s == 0 else middle.at[r, s - 1]
                dst = end[r] if s == last else middle.at[r, s]
                some = pl.ds(0, count)
                hops.append(
                    remote(src.at[some], dst.at[some], send.at[r, s], recv.at[r, s], hist=device)
                )
            ready.append(hops)
        return ready

    far_moves = chain(stage_far, far, far_end, far_room, far_send, far_recv, ahead)
    near_moves = chain(stage_near, near, near_end, near_room, near_send, near_recv, behind)

    def step(r, s):
        if s == 0:
            fill(r, stage_far.at[r], planes - half, 0, far_room[0], False)
        else:
            far_moves[r][s - 1].wait_recv()
            fill(r, far.at[r, s - 1], planes - half + s, 0, far_room[s], True)
        far_moves[r][s].start()
        if s < half - 1:
            distance = half - 1 - s
            if s == 0:
                fill(r, stage_near.at[r], distance, 1, near_room[0], False)
            else:
                near_moves[r][s - 1].wait_recv()
                fill(r, near.at[r, s - 1], distance, 1, near_room[s], True)
            near_moves[r][s].start()

    def finish(r):
        near_moves[r][half - 2].wait_recv()
        far_moves[r][half - 1].wait_recv()

        def body(i, carry):
            kind = codes[0, 2, i]
            spot = codes[0, 3, i]
            tile = tabs[r][codes[0, 4, i]]
            other = jnp.where(kind == 1, far_end[r][spot], near_end[r][spot])
            out_ref[i, pl.ds(r * rows, rows)] = jnp.where(kind == 0, tile, other)
            return carry

        lax.fori_loop(0, slots, body, 0, unroll=2)

    def first():
        loads[0].wait()

    events = [(-9, first, ())]
    for r in range(CHUNKS):
        if r:
            events.append((half * (r - 1) + 0.5, pass_on, (moves[r],)))
            events.append((half * (r - 1) + 2.5, across, (moves[r],)))
            events.append((half * r - 0.5, plane_ready, (moves[r],)))
        if r + 1 < CHUNKS:
            events.append((half * (r - 1) + 0.6 if r else -8, begin, (r + 1,)))
        for s in range(half):
            events.append((half * r + STRIDE * s + 0.01 * r, step, (r, s)))
        events.append((half * r + STRIDE * half + 0.7, finish, (r,)))
    for _, act, args in sorted(events, key=lambda e: e[0]):
        act(*args)

    for group in moves + far_moves + near_moves:
        for copy in group:
            copy.wait_send()


def pull(planes, level, far_room, near_room, table, first, codes):
    tiles, chunks, rows, width = table.shape
    slots = tiles
    half = planes // 2
    dma = pltpu.SemaphoreType.DMA
    block = (slots, rows, width)
    hbm = pl.BlockSpec(memory_space=pl.ANY)
    return pl.pallas_call(
        functools.partial(gather_kernel, planes, far_room, near_room),
        out_shape=jax.ShapeDtypeStruct((slots, chunks * rows, width), table.dtype),
        in_specs=[hbm, hbm, pl.BlockSpec(memory_space=pltpu.SMEM)],
        out_specs=pl.BlockSpec(memory_space=pltpu.VMEM),
        scratch_shapes=[
            [pltpu.VMEM((PLANE * tiles, rows, width), table.dtype)] * chunks,
            pltpu.VMEM((chunks,) + block, table.dtype),
            pltpu.VMEM((chunks,) + block, table.dtype),
            pltpu.VMEM((chunks, half - 1) + block, table.dtype),
            pltpu.VMEM((chunks, half - 2) + block, table.dtype),
            [pltpu.VMEM(block, table.dtype)] * chunks,
            [pltpu.VMEM(block, table.dtype)] * chunks,
            dma((chunks,)),
            dma((chunks, 9)),
            dma((chunks, 9)),
            dma((chunks, half)),
            dma((chunks, half)),
            dma((chunks, half - 1)),
            dma((chunks, half - 1)),
        ],
        compiler_params=pltpu.CompilerParams(
            collective_id=2 + level, has_side_effects=True, vmem_limit_bytes=60 << 20
        ),
    )(table, first, codes)


def rooms(planes, slots):
    half = planes // 2
    full = ((slots,) * half, (slots,) * (half - 1))
    if (planes, slots) != (8, 16):
        return [full]
    return [
        ((6, 9, 11, 13), (6, 9, 11)),
        ((7, 10, 12, 14), (7, 10, 12)),
        ((9, 12, 14, 15), (9, 12, 14)),
        full,
    ]


def words_kernel(planes, levels, tiles, owner_ref, offset_ref, words, count, start):
    me, z, y, c, hist = place(planes)
    sign = 1 - 2 * c
    half = planes // 2
    slots = offset_ref.shape[1]

    def parse(k):
        owner = owner_ref[k, 0]
        oz, oy, oc = position(owner)
        turn = lax.rem(oy - y + Y, Y)
        rel = jnp.where(turn == 0, 0, jnp.where(turn == 3, 1, jnp.where(turn == 1, 2, 3)))
        tile = (rel * CORES + jnp.abs(oc - c)) * tiles + offset_ref[0, k]
        away = lax.rem(sign * (z - oz) + planes, planes)
        return oz * (PLANE * tiles) + tile, tile, away

    any_code = parse(0)[0]
    for away in range(planes):
        count[away] = 0

    def tally(k, carry):
        away = parse(k)[2]
        count[away] += 1
        words[0, k] = any_code
        words[1, k] = any_code
        return carry

    lax.fori_loop(0, slots, tally, 0)

    far_order = list(range(half, 0, -1))
    near_order = list(range(half + 1, planes))
    level = jnp.int32(0)
    start[0] = 0
    sums = []
    for order in (far_order, near_order):
        total = jnp.int32(0)
        ends = []
        for away in order:
            start[away] = total
            total = total + count[away]
            ends.append(total)
        sums.append(ends)
    for room in levels[:-1]:
        over = jnp.int32(0)
        for ends, caps in zip(sums, room):
            for end, cap in zip(ends, caps):
                over = jnp.maximum(over, jnp.where(end > cap, 1, 0))
        level = level + over
    words[5, 0] = level

    def put(k, carry):
        code, tile, away = parse(k)
        spot = start[away]
        start[away] = spot + 1
        kind = jnp.where(away == 0, 0, jnp.where(away <= half, 1, 2))
        words[jnp.where(kind == 0, 6, kind - 1), spot] = code
        words[2, k] = kind
        words[3, k] = jnp.where(kind == 0, 0, spot)
        words[4, k] = tile
        return carry

    lax.fori_loop(0, slots, put, 0)


def requests(planes, levels, tiles, owners, offsets):
    smem = pl.BlockSpec(memory_space=pltpu.SMEM)
    return pl.pallas_call(
        functools.partial(words_kernel, planes, levels, tiles),
        out_shape=jax.ShapeDtypeStruct((8, 128), jnp.int32),
        in_specs=[smem, smem],
        out_specs=smem,
        scratch_shapes=[pltpu.SMEM((planes,), jnp.int32), pltpu.SMEM((planes,), jnp.int32)],
    )(owners, offsets)


GROUPS = 3


def layer_kernel(
    planes, reps, relation_ref, pulled_ref, adjacency_ref, features_ref, cotangent_ref, weights_ref,
    fresh_ref, grad_x_ref, grad_w_ref,
    masked, stacked, pre_ref, dpre_ref, product, kept, give, take, y_bufs, x_bufs, y_sum, x_sum,
    x_out, x_in, y_out, y_in, mine, z_out, z_in, share,
    pair_send, pair_recv, y_send, y_recv, x_send, x_recv,
    x_put, x_get, y_put, y_get, z_send, z_recv, share_send, share_recv,
):
    me, z, y, c, hist = place(planes)
    x = lax.axis_index("rep")
    blocks, tile, width = pulled_ref.shape
    mats = weights_ref.shape[0]
    relations = mats - 1
    batch_tiles = features_ref.shape[0] // tile
    per_tile = blocks // batch_tiles
    own_rows = width // (planes * PLANE)
    per = mats // GROUPS
    lanes = width // reps
    piece = planes * own_rows
    hp = piece // 2
    low, high = dpre_ref.dtype, jnp.float32

    right, left, partner = hist(dy=1), hist(dy=-1), hist(dc=1)
    column = [hist(dz=d) for d in range(1, planes)]
    ring = [hist(dy=d) for d in range(1, Y)]
    others = [lax.rem(x + d, reps) for d in range(1, reps)]
    greet(
        [{"hist": d} for d in column + ring + [partner]] + [{"rep": d} for d in others]
    )

    stacked[0] = features_ref[...]
    pack = 2

    def mix(i, carry):
        t, q0 = lax.div(i, relations // pack), lax.rem(i, relations // pack) * pack
        for k in range(per_tile):
            relation = relation_ref[0, t * per_tile + k]
            block = adjacency_ref[t * per_tile + k]
            for p in range(pack):
                masked[p * tile:(p + 1) * tile, k * tile:(k + 1) * tile] = jnp.where(
                    relation == q0 + p, block, jnp.zeros_like(block)
                )
        rhs = pulled_ref[pl.ds(t * per_tile, per_tile)].reshape(per_tile * tile, width)
        total = jnp.dot(masked[...], rhs, preferred_element_type=high).astype(low)
        for p in range(pack):
            stacked[1 + q0 + p, pl.ds(t * tile, tile)] = total[p * tile:(p + 1) * tile]
        return carry

    lax.fori_loop(0, batch_tiles * relations // pack, mix, 0)

    pre_ref[...] = jnp.dot(stacked[0], weights_ref[0], preferred_element_type=high)

    def project(j, carry):
        pre_ref[...] += jnp.dot(stacked[j], weights_ref[j], preferred_element_type=high)
        return carry

    lax.fori_loop(1, mats, project, 0)

    wide_x = features_ref[...].astype(high)
    wide_g = cotangent_ref[...].astype(high)
    pre = pre_ref[...]
    sigma = jax.nn.sigmoid(pre)
    fresh_ref[...] = (wide_x + pre * sigma).astype(fresh_ref.dtype)
    dpre_ref[...] = (wide_g * sigma * (1.0 + pre * (1.0 - sigma))).astype(low)

    pair = [
        remote(give.at[g], take.at[g], pair_send.at[g], pair_recv.at[g], hist=partner)
        for g in range(GROUPS)
    ]

    def products(g):
        def one(i, carry):
            value = lax.dot_general(
                stacked[g * per + i], dpre_ref[...], (((0,), (0,)), ((), ())),
                preferred_element_type=high,
            )
            product[...] = value.reshape(planes, Y, CORES, own_rows, width)
            for yy in range(Y):
                kept[g, yy, i] = product[:, yy, c].reshape(piece, width)
                give[g, yy, i] = product[:, yy, 1 - c].reshape(piece, width).astype(low)
            return carry

        lax.fori_loop(0, per, one, 0)
        pair[g].start()

    def y_part(g, yy, i):
        return kept[g, yy, i, :hp] + take[g, yy, i, :hp].astype(high)

    def x_part(g, xx, i):
        yy, j = lax.div(i, per), lax.rem(i, per)
        some = pl.ds(pl.multiple_of(xx * lanes, lanes), lanes)
        return kept[g, yy, j, hp:, some] + take[g, yy, j, hp:, some].astype(high)

    def around(size, axis, me_on, bufs, send, recv, part, count, result):
        far, to_next, to_prev, half_in, from_prev, from_next = bufs
        nxt, prv = lax.rem(me_on + 1, size), lax.rem(me_on + size - 1, size)
        across_it = lax.rem(me_on + 2, size)
        q = hp // 2
        top, bottom = pl.ds(0, q), pl.ds(q, q)
        to = (
            {"hist": right}, {"hist": left}
        ) if axis == "y" else ({"rep": nxt}, {"rep": prv})

        def turn(g, which, src, dst, device):
            return remote(src, dst, send.at[g, which], recv.at[g, which], **device)

        turns = [
            [
                turn(g, 0, far.at[g, :, top], half_in.at[g, :, top], to[0]),
                turn(g, 1, far.at[g, :, bottom], half_in.at[g, :, bottom], to[1]),
                turn(g, 2, to_next.at[g, :, bottom], from_prev.at[g, :, bottom], to[0]),
                turn(g, 3, to_prev.at[g, :, top], from_next.at[g, :, top], to[1]),
                turn(g, 4, to_next.at[g, :, top], from_prev.at[g, :, top], to[0]),
                turn(g, 5, to_prev.at[g, :, bottom], from_next.at[g, :, bottom], to[1]),
            ]
            for g in range(GROUPS)
        ]

        def first(g):
            def one(i, carry):
                far[g, i] = part(g, across_it, i).astype(low)
                to_next[g, i, bottom] = part(g, nxt, i)[q:].astype(low)
                to_prev[g, i, top] = part(g, prv, i)[:q].astype(low)
                return carry

            lax.fori_loop(0, count, one, 0)
            for m in range(4):
                turns[g][m].start()

        def second(g):
            turns[g][0].wait_recv()
            turns[g][1].wait_recv()

            def one(i, carry):
                up = part(g, nxt, i)[:q] + half_in[g, i, top].astype(high)
                down = part(g, prv, i)[q:] + half_in[g, i, bottom].astype(high)
                to_next[g, i, top] = up.astype(low)
                to_prev[g, i, bottom] = down.astype(low)
                return carry

            lax.fori_loop(0, count, one, 0)
            turns[g][4].start()
            turns[g][5].start()

        def last(g):
            for m in (2, 3, 4, 5):
                turns[g][m].wait_recv()

            def one(i, carry):
                result[g, i] = (
                    part(g, me_on, i)
                    + from_prev[g, i].astype(high)
                    + from_next[g, i].astype(high)
                )
                return carry

            lax.fori_loop(0, count, one, 0)

        return turns, first, second, last

    y_turns, y_first, y_second, y_last = around(
        Y, "y", y, y_bufs, y_send, y_recv, y_part, per, y_sum
    )
    x_turns, x_first, x_second, x_last = around(
        reps, "x", x, x_bufs, x_send, x_recv, x_part, Y * per, x_sum
    )

    def lanes_of(xx):
        return pl.ds(pl.multiple_of(xx * lanes, lanes), lanes)

    x_moves = [
        [
            remote(
                x_out.at[g, d], x_in.at[g, d], x_put.at[g, d], x_get.at[g, d], rep=others[d - 1]
            )
            for d in range(1, reps)
        ]
        for g in range(GROUPS)
    ]
    y_moves = [
        [
            remote(
                y_out.at[g, d], y_in.at[g, d], y_put.at[g, d], y_get.at[g, d], hist=ring[d - 1]
            )
            for d in range(1, Y)
        ]
        for g in range(GROUPS)
    ]

    def swap(g):
        for d in range(1, reps):
            x_out[g, d] = y_sum[g, :, :, lanes_of(others[d - 1])].astype(low)
            x_moves[g][d - 1].start()
        for d in range(1, Y):
            y_out[g, d] = x_sum[g, pl.ds(lax.rem(y + d, Y) * per, per)].astype(low)
            y_moves[g][d - 1].start()

    def join(g):
        total = y_sum[g, :, :, lanes_of(x)]
        for d in range(1, reps):
            x_moves[g][d - 1].wait_recv()
            total = total + x_in[g, d].astype(high)
        for i in range(per):
            mine[0:planes // 2, g * per + i] = total[i].reshape(planes // 2, own_rows, lanes)
        total = x_sum[g, pl.ds(y * per, per)]
        for d in range(1, Y):
            y_moves[g][d - 1].wait_recv()
            total = total + y_in[g, d].astype(high)
        for i in range(per):
            mine[planes // 2:, g * per + i] = total[i].reshape(planes // 2, own_rows, lanes)

    def first(g):
        pair[g].wait_recv()
        y_first(g)
        x_first(g)

    def second(g):
        y_second(g)
        x_second(g)

    def last(g):
        y_last(g)
        x_last(g)
        swap(g)

    def extra():
        grad_x_ref[...] = (
            wide_g
            + lax.dot_general(
                dpre_ref[...], weights_ref[0], (((1,), (1,)), ((), ())),
                preferred_element_type=high,
            )
        ).astype(grad_x_ref.dtype)

    stages = [products, first, second, last, join]
    for step in range(GROUPS + len(stages) - 1):
        for lag, stage in enumerate(stages):
            if 0 <= step - lag < GROUPS:
                stage(step - lag)
        if step == 0:
            extra()

    z_rows = mats * own_rows

    def stage_z(p, carry):
        z_out[p, pl.ds(0, z_rows)] = mine[p].reshape(z_rows, lanes).astype(low)
        return carry

    lax.fori_loop(0, planes, stage_z, 0)
    z_moves = []
    for d in range(1, planes):
        to = lax.rem(z + d, planes)
        copy = remote(
            z_out.at[to], z_in.at[d], z_send.at[d], z_recv.at[d], hist=column[d - 1]
        )
        copy.start()
        z_moves.append(copy)
    total = mine[z].reshape(z_rows, lanes)
    for d in range(1, planes):
        z_moves[d - 1].wait_recv()
        total = total + z_in[d, pl.ds(0, z_rows)].astype(high)

    share[x] = total
    share_moves = []
    for d in range(1, reps):
        copy = remote(
            share.at[x], share.at[x], share_send.at[d], share_recv.at[d], rep=others[d - 1]
        )
        copy.start()
        share_moves.append(copy)
    for copy in share_moves:
        copy.wait_recv()
    for xx in range(reps):
        grad_w_ref[:, :, xx * lanes:(xx + 1) * lanes] = share[xx].reshape(mats, own_rows, lanes)

    for group in [pair, z_moves, share_moves] + y_turns + x_turns + x_moves + y_moves:
        for copy in group:
            copy.wait_send()


def layer(planes, reps, relation, pulled, tiles, features, cotangent, weights):
    mats, width, _ = weights.shape
    batch = features.shape[0]
    blocks, tile, _ = pulled.shape
    per_tile = blocks * tile // batch
    own_rows = width // (planes * PLANE)
    per = mats // GROUPS
    piece = planes * own_rows
    hp = piece // 2
    lanes = width // reps
    z_pad = -(-mats * own_rows // 16) * 16
    low, high = features.dtype, jnp.float32
    dma = pltpu.SemaphoreType.DMA
    vmem = pl.BlockSpec(memory_space=pltpu.VMEM)
    return pl.pallas_call(
        functools.partial(layer_kernel, planes, reps),
        out_shape=(
            jax.ShapeDtypeStruct((batch, width), low),
            jax.ShapeDtypeStruct((batch, width), low),
            jax.ShapeDtypeStruct((mats, own_rows, width), high),
        ),
        in_specs=[pl.BlockSpec(memory_space=pltpu.SMEM)] + [vmem] * 5,
        out_specs=(vmem, vmem, vmem),
        scratch_shapes=[
            pltpu.VMEM((2 * tile, per_tile * tile), low),
            pltpu.VMEM((mats, batch, width), low),
            pltpu.VMEM((batch, width), high),
            pltpu.VMEM((batch, width), low),
            pltpu.VMEM((planes, Y, CORES, own_rows, width), high),
            pltpu.VMEM((GROUPS, Y, per, piece, width), high),
            pltpu.VMEM((GROUPS, Y, per, piece, width), low),
            pltpu.VMEM((GROUPS, Y, per, piece, width), low),
            [pltpu.VMEM((GROUPS, per, hp, width), low)] * 6,
            [pltpu.VMEM((GROUPS, Y * per, hp, lanes), low)] * 6,
            pltpu.VMEM((GROUPS, per, hp, width), high),
            pltpu.VMEM((GROUPS, Y * per, hp, lanes), high),
            pltpu.VMEM((GROUPS, reps, per, hp, lanes), low),
            pltpu.VMEM((GROUPS, reps, per, hp, lanes), low),
            pltpu.VMEM((GROUPS, Y, per, hp, lanes), low),
            pltpu.VMEM((GROUPS, Y, per, hp, lanes), low),
            pltpu.VMEM((planes, mats, own_rows, lanes), high),
            pltpu.VMEM((planes, z_pad, lanes), low),
            pltpu.VMEM((planes, z_pad, lanes), low),
            pltpu.VMEM((reps, mats * own_rows, lanes), high),
            dma((GROUPS,)),
            dma((GROUPS,)),
            dma((GROUPS, 6)),
            dma((GROUPS, 6)),
            dma((GROUPS, 6)),
            dma((GROUPS, 6)),
            dma((GROUPS, reps)),
            dma((GROUPS, reps)),
            dma((GROUPS, Y)),
            dma((GROUPS, Y)),
            dma((planes,)),
            dma((planes,)),
            dma((reps,)),
            dma((reps,)),
        ],
        compiler_params=pltpu.CompilerParams(
            collective_id=1, has_side_effects=True, vmem_limit_bytes=60 << 20
        ),
    )(relation, pulled, tiles, features, cotangent, weights)


def on_device(
    planes, reps, features, history, blk_owner, blk_offset, blk_relation, adjacency, weights, cotangent
):
    tiles = adjacency[0]
    tile_rows = tiles.shape[-1]
    width = weights.shape[-1]
    mats = weights.shape[0]
    table = history.reshape(-1, tile_rows, width)

    tiles_held = table.shape[0]
    table = table.reshape(tiles_held, CHUNKS, tile_rows // CHUNKS, width)
    levels = rooms(planes, blk_offset.shape[1])
    words = requests(planes, levels, tiles_held, blk_owner[0], blk_offset)
    first, codes, top = ask(planes, reps, table, words)
    pulled = lax.switch(
        top[5, 0],
        [
            functools.partial(pull, planes, level, far_room, near_room)
            for level, (far_room, near_room) in enumerate(levels)
        ],
        table, first, codes,
    )
    fresh, grad_x, grad_w = layer(
        planes, reps, blk_relation, pulled, tiles, features[0], cotangent[0], weights
    )
    return fresh[None], grad_x[None], grad_w.reshape(mats, -1)


def solution(mesh):
    planes = mesh.shape["hist"] // PLANE
    in_specs = (
        P("rep", "hist", None),
        P("rep", "hist", None),
        P("rep", "hist", None),
        P("rep", "hist"),
        P("rep", "hist"),
        P("rep", "hist", None, None),
        P(),
        P("rep", "hist", None),
    )
    out_specs = (P("rep", "hist", None), P("rep", "hist", None), P(None, "hist"))
    return jax.shard_map(
        functools.partial(on_device, planes, mesh.shape["rep"]),
        mesh=mesh, in_specs=in_specs, out_specs=out_specs, check_vma=False,
    )
```

```python
import functools

import jax
import jax.numpy as jnp
from jax import lax
from jax.experimental import pallas as pl
from jax.experimental.pallas import tpu as pltpu
from jax.sharding import PartitionSpec as P

Y = 4
CORES = 2
PLANE = Y * CORES
CHUNKS = 8
LEVEL, FAR, NEAR, KIND, SPOT, TILE, SPARE = 0, 16, 32, 48, 64, 80, 96
STRIDE = 3
HELD = 2
BEGIN, PASS, ACROSS = 7.3, 3.5, 1.5


def position(index):
    return lax.div(index, PLANE), lax.rem(lax.div(index, CORES), Y), lax.rem(index, CORES)


def place(plane_count):
    me = lax.axis_index("hist")
    z, y, c = position(me)

    def hist(dz=0, dy=0, dc=0):
        zz = lax.rem(z + dz + plane_count, plane_count)
        yy = lax.rem(y + dy + Y, Y)
        cc = lax.rem(c + dc, CORES)
        return (zz * Y + yy) * CORES + cc

    return me, z, y, c, hist


def remote(src, dst, send, recv, **device):
    return pltpu.make_async_remote_copy(
        src_ref=src,
        dst_ref=dst,
        send_sem=send,
        recv_sem=recv,
        device_id=device,
        device_id_type=pl.DeviceIdType.MESH,
    )


def greet(partners):
    barrier = pltpu.get_barrier_semaphore()
    for device in partners:
        pl.semaphore_signal(
            barrier, inc=1, device_id=device, device_id_type=pl.DeviceIdType.MESH
        )
    return lambda: pl.semaphore_wait(barrier, len(partners))


def plane_moves(part, link, tiles, right, left, partner):
    h = tiles // 2
    return [
        link(0, part(0, 0), part(1, 0), right),
        link(1, part(0, 0), part(2, 0), left),
        link(2, part(0, 0), part(0, 1), partner),
        link(3, part(1, 0, 0, h), part(3, 0, 0, h), right),
        link(4, part(2, 0, h, h), part(3, 0, h, h), left),
        link(5, part(1, 0), part(1, 1), partner),
        link(6, part(2, 0), part(2, 1), partner),
        link(7, part(3, 0, 0, h), part(3, 1, 0, h), partner),
        link(8, part(3, 0, h, h), part(3, 1, h, h), partner),
    ]


def own_out(moves):
    for m in (0, 1, 2):
        moves[m].start()


def pass_on(moves, wait=True):
    if wait:
        moves[0].wait_recv()
    moves[3].start()
    if wait:
        moves[1].wait_recv()
    moves[4].start()
    moves[5].start()
    moves[6].start()


def across(moves):
    moves[3].wait_recv()
    moves[7].start()
    moves[4].wait_recv()
    moves[8].start()


def plane_ready(moves, own=True):
    for m in (2, 5, 6, 7, 8) if own else (5, 6, 7, 8):
        moves[m].wait_recv()


def part_of(ref, tiles):
    def part(rel, core, lo=0, n=tiles):
        return ref.at[pl.ds((rel * CORES + core) * tiles + lo, n)]

    return part


def ask_kernel(
    planes, reps, table_ref, code_ref, tab_ref, codes, level_ref,
    flags, plane_flags, rep_flags, own_sem, load_sem, code_send, code_recv,
    flag_send, flag_recv, top_send, top_recv, ring_send, ring_recv,
):
    me, z, y, c, hist = place(planes)
    sign = 1 - 2 * c
    x = lax.axis_index("rep")
    tiles = table_ref.shape[0]
    right, left, partner = hist(dy=1), hist(dy=-1), hist(dc=1)
    column = [hist(dz=sign * d) for d in range(1, planes)]
    plane = [hist(dy=d // CORES, dc=d % CORES) for d in range(1, PLANE)]
    others = [lax.rem(x + d, reps) for d in range(1, reps)]
    all_here = greet(
        [{"hist": d} for d in column + plane] + [{"rep": d} for d in others]
    )
    parts = [part_of(tab_ref.at[r], tiles) for r in range(HELD)]
    loads = [
        pltpu.make_async_copy(table_ref.at[:, r], parts[r](0, 0), load_sem.at[r])
        for r in range(HELD)
    ]
    for copy in loads:
        copy.start()
    all_here()

    own = pltpu.make_async_copy(code_ref, codes.at[0], own_sem)
    own.start()
    asks = []
    for d in range(1, planes):
        copy = remote(
            code_ref, codes.at[d], code_send.at[d], code_recv.at[d], hist=column[d - 1]
        )
        copy.start()
        asks.append(copy)

    moves = []
    for r in range(HELD):
        def link(which, src, dst, device, r=r):
            return remote(
                src, dst, ring_send.at[r, which], ring_recv.at[r, which], hist=device
            )

        moves.append(plane_moves(parts[r], link, tiles, right, left, partner))
        loads[r].wait()
        if r == 0:
            own_out(moves[0])

    own.wait()
    for copy in asks:
        copy.wait_recv()
    top = codes[0]
    for d in range(1, planes):
        top = jnp.maximum(top, codes[d])
    flags[0] = top
    spread = []
    for d in range(1, PLANE):
        copy = remote(
            flags.at[0], plane_flags.at[d], flag_send.at[d], flag_recv.at[d], hist=plane[d - 1]
        )
        copy.start()
        spread.append(copy)
    pass_on(moves[0])
    own_out(moves[1])
    for d in range(1, PLANE):
        spread[d - 1].wait_recv()
        top = jnp.maximum(top, plane_flags[d])
    flags[1] = top
    over = []
    for d in range(1, reps):
        copy = remote(
            flags.at[1], rep_flags.at[d], top_send.at[d], top_recv.at[d], rep=others[d - 1]
        )
        copy.start()
        over.append(copy)
    across(moves[0])
    for d in range(1, reps):
        over[d - 1].wait_recv()
        top = jnp.maximum(top, rep_flags[d])
    level_ref[0, 0] = top[0, 0]

    plane_ready(moves[0])
    for m in (0, 1, 2):
        moves[1][m].wait_recv()
    for group in [asks, spread, over, moves[0], moves[1][:3]]:
        for copy in group:
            copy.wait_send()


def ask(planes, reps, table, code):
    tiles, chunks, rows, width = table.shape
    dma = pltpu.SemaphoreType.DMA
    vmem = pl.BlockSpec(memory_space=pltpu.VMEM)
    words = pltpu.VMEM
    return pl.pallas_call(
        functools.partial(ask_kernel, planes, reps),
        out_shape=(
            jax.ShapeDtypeStruct((HELD, PLANE * tiles, rows, width), table.dtype),
            jax.ShapeDtypeStruct((planes, 1, 128), jnp.int32),
            jax.ShapeDtypeStruct((1, 1), jnp.int32),
        ),
        in_specs=[pl.BlockSpec(memory_space=pl.ANY), vmem],
        out_specs=(vmem, vmem, pl.BlockSpec(memory_space=pltpu.SMEM)),
        scratch_shapes=[
            words((2, 1, 128), jnp.int32),
            words((PLANE, 1, 128), jnp.int32),
            words((reps, 1, 128), jnp.int32),
            dma(()),
            dma((HELD,)),
            dma((planes,)),
            dma((planes,)),
            dma((PLANE,)),
            dma((PLANE,)),
            dma((reps,)),
            dma((reps,)),
            dma((HELD, 9)),
            dma((HELD, 9)),
        ],
        compiler_params=pltpu.CompilerParams(collective_id=0, has_side_effects=True, vmem_limit_bytes=16 << 20),
    )(table, code)


def gather_kernel(
    planes, far_room, near_room, table_ref, first_ref, codes, out_ref,
    tabs, stage_far, stage_near, far, near, far_end, near_end,
    load_sem, ring_send, ring_recv, far_send, far_recv, near_send, near_recv,
):
    me, z, y, c, hist = place(planes)
    sign = 1 - 2 * c
    half = planes // 2
    tiles = table_ref.shape[0]
    rows = table_ref.shape[2]
    slots = out_ref.shape[0]

    right, left, partner = hist(dy=1), hist(dy=-1), hist(dc=1)
    ahead, behind = hist(dz=sign), hist(dz=-sign)
    all_here = greet([{"hist": d} for d in (right, left, partner, ahead, behind)])
    most, one = pl.ds(0, 3 * tiles), pl.ds(4 * tiles, tiles)
    loads = [
        [pltpu.make_async_copy(first_ref.at[0], tabs[0], load_sem.at[0])],
        [
            pltpu.make_async_copy(first_ref.at[1, most], tabs[1].at[most], load_sem.at[1]),
            pltpu.make_async_copy(first_ref.at[1, one], tabs[1].at[one], load_sem.at[CHUNKS]),
        ],
    ] + [
        [
            pltpu.make_async_copy(
                table_ref.at[:, r], tabs[r].at[pl.ds(0, tiles)], load_sem.at[r]
            )
        ]
        for r in range(HELD, CHUNKS)
    ]
    for copies in loads:
        for copy in copies:
            copy.start()

    def loaded(r):
        for copy in loads[r]:
            copy.wait()

    moves = [[]]
    for r in range(1, CHUNKS):
        def link(which, src, dst, device, r=r):
            return remote(
                src, dst, ring_send.at[r, which], ring_recv.at[r, which], hist=device
            )

        moves.append(plane_moves(part_of(tabs[r], tiles), link, tiles, right, left, partner))

    def begin(r):
        loaded(r)
        own_out(moves[r])

    def second():
        loaded(1)
        pass_on(moves[1], False)

    def fill(r, dst, slot, lane, count, merge):
        def body(i, carry):
            code = codes[slot, 0, lane + i]
            tile = tabs[r][lax.rem(code, PLANE * tiles)]
            if merge:
                tile = jnp.where(lax.div(code, PLANE * tiles) == z, tile, dst[i])
            dst[i] = tile
            return carry

        lax.fori_loop(0, count, body, 0, unroll=2)

    def chain(stage, middle, end, room, send, recv, device):
        last = len(room) - 1
        ready = []
        for r in range(CHUNKS):
            hops = []
            for s, count in enumerate(room):
                src = stage.at[r] if s == 0 else middle.at[r, s - 1]
                dst = end[r] if s == last else middle.at[r, s]
                some = pl.ds(0, count)
                hops.append(
                    remote(src.at[some], dst.at[some], send.at[r, s], recv.at[r, s], hist=device)
                )
            ready.append(hops)
        return ready

    far_moves = chain(stage_far, far, far_end, far_room, far_send, far_recv, ahead)
    near_moves = chain(stage_near, near, near_end, near_room, near_send, near_recv, behind)

    def step(r, s):
        if s == 0:
            fill(r, stage_far.at[r], planes - half, FAR, far_room[0], False)
        else:
            far_moves[r][s - 1].wait_recv()
            fill(r, far.at[r, s - 1], planes - half + s, FAR, far_room[s], True)
        far_moves[r][s].start()
        if s < half - 1:
            distance = half - 1 - s
            if s == 0:
                fill(r, stage_near.at[r], distance, NEAR, near_room[0], False)
            else:
                near_moves[r][s - 1].wait_recv()
                fill(r, near.at[r, s - 1], distance, NEAR, near_room[s], True)
            near_moves[r][s].start()

    def finish(r):
        near_moves[r][half - 2].wait_recv()
        far_moves[r][half - 1].wait_recv()

        def body(i, carry):
            kind = codes[0, 0, KIND + i]
            spot = codes[0, 0, SPOT + i]
            tile = tabs[r][codes[0, 0, TILE + i]]
            other = jnp.where(kind == 1, far_end[r][spot], near_end[r][spot])
            out_ref[i, pl.ds(r * rows, rows)] = jnp.where(kind == 0, tile, other)
            return carry

        lax.fori_loop(0, slots, body, 0, unroll=2)

    events = [(-7, all_here, ()), (-5, second, ()), (-0.5, loaded, (0,))]
    for r in range(CHUNKS):
        if r >= HELD:
            events.append((half * r - BEGIN, begin, (r,)))
            events.append((half * r - PASS, pass_on, (moves[r],)))
        if r:
            events.append((half * r - ACROSS, across, (moves[r],)))
            events.append((half * r - 0.5, plane_ready, (moves[r], r >= HELD)))
        for s in range(half):
            events.append((half * r + STRIDE * s + 0.01 * r, step, (r, s)))
        events.append((half * r + STRIDE * half + 0.7, finish, (r,)))
    for _, act, args in sorted(events, key=lambda e: e[0]):
        act(*args)

    for group in [moves[1][3:]] + moves[HELD:] + far_moves + near_moves:
        for copy in group:
            copy.wait_send()


def pull(planes, level, far_room, near_room, table, first, codes):
    tiles, chunks, rows, width = table.shape
    slots = tiles
    half = planes // 2
    dma = pltpu.SemaphoreType.DMA
    block = (slots, rows, width)
    hbm = pl.BlockSpec(memory_space=pl.ANY)
    return pl.pallas_call(
        functools.partial(gather_kernel, planes, far_room, near_room),
        out_shape=jax.ShapeDtypeStruct((slots, chunks * rows, width), table.dtype),
        in_specs=[hbm, hbm, pl.BlockSpec(memory_space=pltpu.SMEM)],
        out_specs=pl.BlockSpec(memory_space=pltpu.VMEM),
        scratch_shapes=[
            [pltpu.VMEM((PLANE * tiles, rows, width), table.dtype)] * chunks,
            pltpu.VMEM((chunks,) + block, table.dtype),
            pltpu.VMEM((chunks,) + block, table.dtype),
            pltpu.VMEM((chunks, half - 1) + block, table.dtype),
            pltpu.VMEM((chunks, half - 2) + block, table.dtype),
            [pltpu.VMEM(block, table.dtype)] * chunks,
            [pltpu.VMEM(block, table.dtype)] * chunks,
            dma((chunks + 1,)),
            dma((chunks, 9)),
            dma((chunks, 9)),
            dma((chunks, half)),
            dma((chunks, half)),
            dma((chunks, half - 1)),
            dma((chunks, half - 1)),
        ],
        compiler_params=pltpu.CompilerParams(
            collective_id=2 + level, has_side_effects=True, vmem_limit_bytes=60 << 20
        ),
    )(table, first, codes)


def rooms(planes, slots):
    half = planes // 2
    full = ((slots,) * half, (slots,) * (half - 1))
    if (planes, slots) != (8, 16):
        return [full]
    return [
        ((6, 9, 11, 13), (6, 9, 11)),
        ((7, 10, 12, 14), (7, 10, 12)),
        ((9, 12, 14, 15), (9, 12, 14)),
        full,
    ]


def words_kernel(planes, levels, tiles, owner_ref, offset_ref, words, count, start):
    me, z, y, c, hist = place(planes)
    sign = 1 - 2 * c
    half = planes // 2
    slots = offset_ref.shape[1]

    def parse(k):
        owner = owner_ref[0, k]
        oz, oy, oc = position(owner)
        turn = lax.rem(oy - y + Y, Y)
        rel = jnp.where(turn == 0, 0, jnp.where(turn == 3, 1, jnp.where(turn == 1, 2, 3)))
        tile = (rel * CORES + jnp.abs(oc - c)) * tiles + offset_ref[0, k]
        away = lax.rem(sign * (z - oz) + planes, planes)
        return oz * (PLANE * tiles) + tile, tile, away

    any_code = parse(0)[0]
    for away in range(planes):
        count[away] = 0

    def tally(k, carry):
        away = parse(k)[2]
        count[away] += 1
        words[0, FAR + k] = any_code
        words[0, NEAR + k] = any_code
        return carry

    lax.fori_loop(0, slots, tally, 0)

    far_order = list(range(half, 0, -1))
    near_order = list(range(half + 1, planes))
    level = jnp.int32(0)
    start[0] = 0
    sums = []
    for order in (far_order, near_order):
        total = jnp.int32(0)
        ends = []
        for away in order:
            start[away] = total
            total = total + count[away]
            ends.append(total)
        sums.append(ends)
    for room in levels[:-1]:
        over = jnp.int32(0)
        for ends, caps in zip(sums, room):
            for end, cap in zip(ends, caps):
                over = jnp.maximum(over, jnp.where(end > cap, 1, 0))
        level = level + over
    words[0, LEVEL] = level

    def put(k, carry):
        code, tile, away = parse(k)
        spot = start[away]
        start[away] = spot + 1
        kind = jnp.where(away == 0, 0, jnp.where(away <= half, 1, 2))
        words[0, jnp.where(kind == 0, SPARE, jnp.where(kind == 1, FAR, NEAR)) + spot] = code
        words[0, KIND + k] = kind
        words[0, SPOT + k] = jnp.where(kind == 0, 0, spot)
        words[0, TILE + k] = tile
        return carry

    lax.fori_loop(0, slots, put, 0)


def requests(planes, levels, tiles, owners, offsets):
    smem = pl.BlockSpec(memory_space=pltpu.SMEM)
    return pl.pallas_call(
        functools.partial(words_kernel, planes, levels, tiles),
        out_shape=jax.ShapeDtypeStruct((1, 128), jnp.int32),
        in_specs=[smem, smem],
        out_specs=smem,
        scratch_shapes=[pltpu.SMEM((planes,), jnp.int32), pltpu.SMEM((planes,), jnp.int32)],
    )(owners, offsets)


GROUPS = 3
LAG = 1.1


def layer_kernel(
    planes, reps, relation_ref, pulled_ref, adjacency_ref, features_ref, cotangent_ref, weights_ref,
    fresh_ref, grad_x_ref, grad_w_ref,
    masked, stacked, pre_ref, dpre_ref, product, kept, give, take, y_bufs, x_bufs, y_sum, x_sum,
    x_out, x_in, y_out, y_in, mine, z_out, z_in, share,
    pair_send, pair_recv, y_send, y_recv, x_send, x_recv,
    x_put, x_get, y_put, y_get, z_send, z_recv, share_send, share_recv, weights_held, weights_sem,
):
    me, z, y, c, hist = place(planes)
    x = lax.axis_index("rep")
    blocks, tile, width = pulled_ref.shape
    mats = weights_ref.shape[0]
    relations = mats - 1
    batch_tiles = features_ref.shape[0] // tile
    per_tile = blocks // batch_tiles
    own_rows = width // (planes * PLANE)
    per = mats // GROUPS
    lanes = width // reps
    piece = planes * own_rows
    hp = piece // 2
    low, high = dpre_ref.dtype, jnp.float32

    right, left, partner = hist(dy=1), hist(dy=-1), hist(dc=1)
    column = [hist(dz=d) for d in range(1, planes)]
    ring = [hist(dy=d) for d in range(1, Y)]
    others = [lax.rem(x + d, reps) for d in range(1, reps)]
    all_here = greet(
        [{"hist": d} for d in column + ring + [partner]] + [{"rep": d} for d in others]
    )
    fetch = pltpu.make_async_copy(weights_ref, weights_held, weights_sem)
    fetch.start()

    stacked[0] = features_ref[...]
    pack = 2

    def mix(i, carry):
        t, q0 = lax.div(i, relations // pack), lax.rem(i, relations // pack) * pack
        for k in range(per_tile):
            relation = relation_ref[0, t * per_tile + k]
            block = adjacency_ref[t * per_tile + k]
            for p in range(pack):
                masked[p * tile:(p + 1) * tile, k * tile:(k + 1) * tile] = jnp.where(
                    relation == q0 + p, block, jnp.zeros_like(block)
                )
        rhs = pulled_ref[pl.ds(t * per_tile, per_tile)].reshape(per_tile * tile, width)
        total = jnp.dot(masked[...], rhs, preferred_element_type=high).astype(low)
        for p in range(pack):
            stacked[1 + q0 + p, pl.ds(t * tile, tile)] = total[p * tile:(p + 1) * tile]
        return carry

    lax.fori_loop(0, batch_tiles * relations // pack, mix, 0)

    fetch.wait()
    pre_ref[...] = jnp.dot(stacked[0], weights_held[0], preferred_element_type=high)

    def project(j, carry):
        pre_ref[...] += jnp.dot(stacked[j], weights_held[j], preferred_element_type=high)
        return carry

    lax.fori_loop(1, mats, project, 0)

    wide_x = features_ref[...].astype(high)
    wide_g = cotangent_ref[...].astype(high)
    pre = pre_ref[...]
    sigma = jax.nn.sigmoid(pre)
    fresh_ref[...] = (wide_x + pre * sigma).astype(fresh_ref.dtype)
    dpre_ref[...] = (wide_g * sigma * (1.0 + pre * (1.0 - sigma))).astype(low)

    pair = [
        remote(give.at[g], take.at[g], pair_send.at[g], pair_recv.at[g], hist=partner)
        for g in range(GROUPS)
    ]

    def products(g):
        def one(i, carry):
            value = lax.dot_general(
                stacked[g * per + i], dpre_ref[...], (((0,), (0,)), ((), ())),
                preferred_element_type=high,
            )
            product[...] = value.reshape(planes, Y, CORES, own_rows, width)
            for yy in range(Y):
                kept[g, yy, i] = product[:, yy, c].reshape(piece, width)
                give[g, yy, i] = product[:, yy, 1 - c].reshape(piece, width).astype(low)
            return carry

        lax.fori_loop(0, per, one, 0)
        pair[g].start()

    def y_part(g, yy, i):
        return kept[g, yy, i, :hp] + take[g, yy, i, :hp].astype(high)

    def x_part(g, xx, i):
        yy, j = lax.div(i, per), lax.rem(i, per)
        some = pl.ds(pl.multiple_of(xx * lanes, lanes), lanes)
        return kept[g, yy, j, hp:, some] + take[g, yy, j, hp:, some].astype(high)

    def around(size, axis, me_on, bufs, send, recv, part, count, result):
        far, to_next, to_prev, half_in, from_prev, from_next = bufs
        nxt, prv = lax.rem(me_on + 1, size), lax.rem(me_on + size - 1, size)
        across_it = lax.rem(me_on + 2, size)
        q = hp // 2
        top, bottom = pl.ds(0, q), pl.ds(q, q)
        to = (
            {"hist": right}, {"hist": left}
        ) if axis == "y" else ({"rep": nxt}, {"rep": prv})

        def turn(g, which, src, dst, device):
            return remote(src, dst, send.at[g, which], recv.at[g, which], **device)

        turns = [
            [
                turn(g, 0, far.at[g, :, top], half_in.at[g, :, top], to[0]),
                turn(g, 1, far.at[g, :, bottom], half_in.at[g, :, bottom], to[1]),
                turn(g, 2, to_next.at[g, :, bottom], from_prev.at[g, :, bottom], to[0]),
                turn(g, 3, to_prev.at[g, :, top], from_next.at[g, :, top], to[1]),
                turn(g, 4, to_next.at[g, :, top], from_prev.at[g, :, top], to[0]),
                turn(g, 5, to_prev.at[g, :, bottom], from_next.at[g, :, bottom], to[1]),
            ]
            for g in range(GROUPS)
        ]

        def first(g):
            def one(i, carry):
                far[g, i] = part(g, across_it, i).astype(low)
                to_next[g, i, bottom] = part(g, nxt, i)[q:].astype(low)
                to_prev[g, i, top] = part(g, prv, i)[:q].astype(low)
                return carry

            lax.fori_loop(0, count, one, 0)
            for m in range(4):
                turns[g][m].start()

        def second(g):
            turns[g][0].wait_recv()
            turns[g][1].wait_recv()

            def one(i, carry):
                up = part(g, nxt, i)[:q] + half_in[g, i, top].astype(high)
                down = part(g, prv, i)[q:] + half_in[g, i, bottom].astype(high)
                to_next[g, i, top] = up.astype(low)
                to_prev[g, i, bottom] = down.astype(low)
                return carry

            lax.fori_loop(0, count, one, 0)
            turns[g][4].start()
            turns[g][5].start()

        def last(g):
            for m in (2, 3, 4, 5):
                turns[g][m].wait_recv()

            def one(i, carry):
                result[g, i] = (
                    part(g, me_on, i)
                    + from_prev[g, i].astype(high)
                    + from_next[g, i].astype(high)
                )
                return carry

            lax.fori_loop(0, count, one, 0)

        return turns, first, second, last

    y_turns, y_first, y_second, y_last = around(
        Y, "y", y, y_bufs, y_send, y_recv, y_part, per, y_sum
    )
    x_turns, x_first, x_second, x_last = around(
        reps, "x", x, x_bufs, x_send, x_recv, x_part, Y * per, x_sum
    )

    def lanes_of(xx):
        return pl.ds(pl.multiple_of(xx * lanes, lanes), lanes)

    x_moves = [
        [
            remote(
                x_out.at[g, d], x_in.at[g, d], x_put.at[g, d], x_get.at[g, d], rep=others[d - 1]
            )
            for d in range(1, reps)
        ]
        for g in range(GROUPS)
    ]
    y_moves = [
        [
            remote(
                y_out.at[g, d], y_in.at[g, d], y_put.at[g, d], y_get.at[g, d], hist=ring[d - 1]
            )
            for d in range(1, Y)
        ]
        for g in range(GROUPS)
    ]

    def swap(g):
        for d in range(1, reps):
            x_out[g, d] = y_sum[g, :, :, lanes_of(others[d - 1])].astype(low)
            x_moves[g][d - 1].start()
        for d in range(1, Y):
            y_out[g, d] = x_sum[g, pl.ds(lax.rem(y + d, Y) * per, per)].astype(low)
            y_moves[g][d - 1].start()

    def join(g):
        total = y_sum[g, :, :, lanes_of(x)]
        for d in range(1, reps):
            x_moves[g][d - 1].wait_recv()
            total = total + x_in[g, d].astype(high)
        for i in range(per):
            mine[0:planes // 2, g * per + i] = total[i].reshape(planes // 2, own_rows, lanes)
        total = x_sum[g, pl.ds(y * per, per)]
        for d in range(1, Y):
            y_moves[g][d - 1].wait_recv()
            total = total + y_in[g, d].astype(high)
        for i in range(per):
            mine[planes // 2:, g * per + i] = total[i].reshape(planes // 2, own_rows, lanes)

    def first(g):
        pair[g].wait_recv()
        y_first(g)
        x_first(g)

    def second(g):
        y_second(g)
        x_second(g)

    def last(g):
        y_last(g)
        x_last(g)
        swap(g)

    def extra():
        grad_x_ref[...] = (
            wide_g
            + lax.dot_general(
                dpre_ref[...], weights_held[0], (((1,), (1,)), ((), ())),
                preferred_element_type=high,
            )
        ).astype(grad_x_ref.dtype)

    all_here()
    stages = [products, first, second, last, join]
    extra_at = [(GROUPS - 0.5, -1, extra, ())]
    timed = [
        (g + LAG * lag, -lag, stage, (g,))
        for lag, stage in enumerate(stages)
        for g in range(GROUPS)
    ]
    for _, _, act, args in sorted(timed + extra_at, key=lambda e: e[:2]):
        act(*args)

    z_rows = mats * own_rows

    def stage_z(p, carry):
        z_out[p, pl.ds(0, z_rows)] = mine[p].reshape(z_rows, lanes).astype(low)
        return carry

    lax.fori_loop(0, planes, stage_z, 0)
    z_moves = []
    for d in range(1, planes):
        to = lax.rem(z + d, planes)
        copy = remote(
            z_out.at[to], z_in.at[d], z_send.at[d], z_recv.at[d], hist=column[d - 1]
        )
        copy.start()
        z_moves.append(copy)
    total = mine[z].reshape(z_rows, lanes)
    for d in range(1, planes):
        z_moves[d - 1].wait_recv()
        total = total + z_in[d, pl.ds(0, z_rows)].astype(high)

    share[x] = total
    share_moves = []
    for d in range(1, reps):
        copy = remote(
            share.at[x], share.at[x], share_send.at[d], share_recv.at[d], rep=others[d - 1]
        )
        copy.start()
        share_moves.append(copy)
    for copy in share_moves:
        copy.wait_recv()
    for i in range(own_rows):
        for xx in range(reps):
            at = i * width + xx * lanes
            grad_w_ref[:, at:at + lanes] = share[xx, pl.ds(i, mats, stride=own_rows)]

    for group in [pair, z_moves, share_moves] + y_turns + x_turns + x_moves + y_moves:
        for copy in group:
            copy.wait_send()


def layer(planes, reps, relation, pulled, tiles, features, cotangent, weights):
    mats, width, _ = weights.shape
    batch = features.shape[0]
    blocks, tile, _ = pulled.shape
    per_tile = blocks * tile // batch
    own_rows = width // (planes * PLANE)
    per = mats // GROUPS
    piece = planes * own_rows
    hp = piece // 2
    lanes = width // reps
    z_pad = -(-mats * own_rows // 16) * 16
    low, high = features.dtype, jnp.float32
    dma = pltpu.SemaphoreType.DMA
    vmem = pl.BlockSpec(memory_space=pltpu.VMEM)
    return pl.pallas_call(
        functools.partial(layer_kernel, planes, reps),
        out_shape=(
            jax.ShapeDtypeStruct((batch, width), low),
            jax.ShapeDtypeStruct((batch, width), low),
            jax.ShapeDtypeStruct((mats, own_rows * width), high),
        ),
        in_specs=[pl.BlockSpec(memory_space=pltpu.SMEM)] + [vmem] * 4 + [pl.BlockSpec(memory_space=pl.ANY)],
        out_specs=(vmem, vmem, vmem),
        scratch_shapes=[
            pltpu.VMEM((2 * tile, per_tile * tile), low),
            pltpu.VMEM((mats, batch, width), low),
            pltpu.VMEM((batch, width), high),
            pltpu.VMEM((batch, width), low),
            pltpu.VMEM((planes, Y, CORES, own_rows, width), high),
            pltpu.VMEM((GROUPS, Y, per, piece, width), high),
            pltpu.VMEM((GROUPS, Y, per, piece, width), low),
            pltpu.VMEM((GROUPS, Y, per, piece, width), low),
            [pltpu.VMEM((GROUPS, per, hp, width), low)] * 6,
            [pltpu.VMEM((GROUPS, Y * per, hp, lanes), low)] * 6,
            pltpu.VMEM((GROUPS, per, hp, width), high),
            pltpu.VMEM((GROUPS, Y * per, hp, lanes), high),
            pltpu.VMEM((GROUPS, reps, per, hp, lanes), low),
            pltpu.VMEM((GROUPS, reps, per, hp, lanes), low),
            pltpu.VMEM((GROUPS, Y, per, hp, lanes), low),
            pltpu.VMEM((GROUPS, Y, per, hp, lanes), low),
            pltpu.VMEM((planes, mats, own_rows, lanes), high),
            pltpu.VMEM((planes, z_pad, lanes), low),
            pltpu.VMEM((planes, z_pad, lanes), low),
            pltpu.VMEM((reps, mats * own_rows, lanes), high),
            dma((GROUPS,)),
            dma((GROUPS,)),
            dma((GROUPS, 6)),
            dma((GROUPS, 6)),
            dma((GROUPS, 6)),
            dma((GROUPS, 6)),
            dma((GROUPS, reps)),
            dma((GROUPS, reps)),
            dma((GROUPS, Y)),
            dma((GROUPS, Y)),
            dma((planes,)),
            dma((planes,)),
            dma((reps,)),
            dma((reps,)),
            pltpu.VMEM(weights.shape, low),
            dma(()),
        ],
        compiler_params=pltpu.CompilerParams(
            collective_id=1, has_side_effects=True, vmem_limit_bytes=60 << 20
        ),
    )(relation, pulled, tiles, features, cotangent, weights)


def hand_over_kernel(a_ref, b_ref, c_ref, a_out, b_out, c_out):
    a_out[...] = a_ref[...]
    b_out[...] = b_ref[...]
    c_out[...] = c_ref[...]


def hand_over(*results):
    vmem = pl.BlockSpec(memory_space=pltpu.VMEM)
    return pl.pallas_call(
        hand_over_kernel,
        out_shape=tuple(jax.ShapeDtypeStruct(r.shape, r.dtype) for r in results),
        in_specs=[vmem] * 3,
        out_specs=(vmem,) * 3,
    )(*results)


def on_device(
    planes, reps, features, history, blk_owner, blk_offset, blk_relation, adjacency, weights, cotangent
):
    tiles = adjacency[0]
    tile_rows = tiles.shape[-1]
    width = weights.shape[-1]
    mats = weights.shape[0]
    table = history.reshape(-1, tile_rows, width)

    tiles_held = table.shape[0]
    table = table.reshape(tiles_held, CHUNKS, tile_rows // CHUNKS, width)
    levels = rooms(planes, blk_offset.shape[1])
    words = requests(planes, levels, tiles_held, blk_owner.reshape(1, -1), blk_offset)
    first, codes, top = ask(planes, reps, table, words)
    pulled = lax.switch(
        top[0, 0],
        [
            functools.partial(pull, planes, level, far_room, near_room)
            for level, (far_room, near_room) in enumerate(levels)
        ],
        table, first, codes,
    )
    fresh, grad_x, grad_w = layer(
        planes, reps, blk_relation, pulled, tiles, features[0], cotangent[0], weights
    )
    fresh, grad_x, grad_w = hand_over(fresh, grad_x, grad_w)
    return fresh[None], grad_x[None], grad_w


def solution(mesh):
    planes = mesh.shape["hist"] // PLANE
    in_specs = (
        P("rep", "hist", None),
        P("rep", "hist", None),
        P("rep", "hist", None),
        P("rep", "hist"),
        P("rep", "hist"),
        P("rep", "hist", None, None),
        P(),
        P("rep", "hist", None),
    )
    out_specs = (P("rep", "hist", None), P("rep", "hist", None), P(None, "hist"))
    return jax.shard_map(
        functools.partial(on_device, planes, mesh.shape["rep"]),
        mesh=mesh, in_specs=in_specs, out_specs=out_specs, check_vma=False,
    )
```

```python
import functools

import jax
import jax.numpy as jnp
from jax import lax
from jax.experimental import pallas as pl
from jax.experimental.pallas import tpu as pltpu
from jax.sharding import PartitionSpec as P

Y = 4
CORES = 2
PLANE = Y * CORES
CHUNKS = 8
LEVEL, FAR, NEAR, KIND, SPOT, TILE, SPARE = 0, 16, 32, 48, 64, 80, 96
STRIDE = 3
HELD = 2
BEGIN, PASS, ACROSS = 7.3, 3.5, 1.5


def position(index):
    return lax.div(index, PLANE), lax.rem(lax.div(index, CORES), Y), lax.rem(index, CORES)


def place(plane_count):
    me = lax.axis_index("hist")
    z, y, c = position(me)

    def hist(dz=0, dy=0, dc=0):
        zz = lax.rem(z + dz + plane_count, plane_count)
        yy = lax.rem(y + dy + Y, Y)
        cc = lax.rem(c + dc, CORES)
        return (zz * Y + yy) * CORES + cc

    return me, z, y, c, hist


def remote(src, dst, send, recv, **device):
    return pltpu.make_async_remote_copy(
        src_ref=src,
        dst_ref=dst,
        send_sem=send,
        recv_sem=recv,
        device_id=device,
        device_id_type=pl.DeviceIdType.MESH,
    )


def greet(partners):
    barrier = pltpu.get_barrier_semaphore()
    for device in partners:
        pl.semaphore_signal(
            barrier, inc=1, device_id=device, device_id_type=pl.DeviceIdType.MESH
        )
    return lambda: pl.semaphore_wait(barrier, len(partners))


def plane_moves(part, link, tiles, right, left, partner):
    h = tiles // 2
    return [
        link(0, part(0, 0), part(1, 0), right),
        link(1, part(0, 0), part(2, 0), left),
        link(2, part(0, 0), part(0, 1), partner),
        link(3, part(1, 0, 0, h), part(3, 0, 0, h), right),
        link(4, part(2, 0, h, h), part(3, 0, h, h), left),
        link(5, part(1, 0), part(1, 1), partner),
        link(6, part(2, 0), part(2, 1), partner),
        link(7, part(3, 0, 0, h), part(3, 1, 0, h), partner),
        link(8, part(3, 0, h, h), part(3, 1, h, h), partner),
    ]


def own_out(moves):
    for m in (0, 1, 2):
        moves[m].start()


def pass_on(moves, wait=True):
    if wait:
        moves[0].wait_recv()
    moves[3].start()
    if wait:
        moves[1].wait_recv()
    moves[4].start()
    moves[5].start()
    moves[6].start()


def across(moves):
    moves[3].wait_recv()
    moves[7].start()
    moves[4].wait_recv()
    moves[8].start()


def plane_ready(moves, own=True):
    for m in (2, 5, 6, 7, 8) if own else (5, 6, 7, 8):
        moves[m].wait_recv()


def part_of(ref, tiles):
    def part(rel, core, lo=0, n=tiles):
        return ref.at[pl.ds((rel * CORES + core) * tiles + lo, n)]

    return part


def ask_kernel(
    planes, reps, table_ref, code_ref, tab_ref, codes, level_ref,
    flags, plane_flags, rep_flags, own_sem, load_sem, code_send, code_recv,
    flag_send, flag_recv, top_send, top_recv, ring_send, ring_recv,
):
    me, z, y, c, hist = place(planes)
    sign = 1 - 2 * c
    x = lax.axis_index("rep")
    tiles = table_ref.shape[0]
    right, left, partner = hist(dy=1), hist(dy=-1), hist(dc=1)
    column = [hist(dz=sign * d) for d in range(1, planes)]
    plane = [hist(dy=d // CORES, dc=d % CORES) for d in range(1, PLANE)]
    others = [lax.rem(x + d, reps) for d in range(1, reps)]
    all_here = greet(
        [{"hist": d} for d in column + plane] + [{"rep": d} for d in others]
    )
    parts = [part_of(tab_ref.at[r], tiles) for r in range(HELD)]
    loads = [
        pltpu.make_async_copy(table_ref.at[:, r], parts[r](0, 0), load_sem.at[r])
        for r in range(HELD)
    ]
    for copy in loads:
        copy.start()
    all_here()

    own = pltpu.make_async_copy(code_ref, codes.at[0], own_sem)
    own.start()
    asks = []
    for d in range(1, planes):
        copy = remote(
            code_ref, codes.at[d], code_send.at[d], code_recv.at[d], hist=column[d - 1]
        )
        copy.start()
        asks.append(copy)

    moves = []
    for r in range(HELD):
        def link(which, src, dst, device, r=r):
            return remote(
                src, dst, ring_send.at[r, which], ring_recv.at[r, which], hist=device
            )

        moves.append(plane_moves(parts[r], link, tiles, right, left, partner))
        loads[r].wait()
        if r == 0:
            own_out(moves[0])

    own.wait()
    for copy in asks:
        copy.wait_recv()
    top = codes[0]
    for d in range(1, planes):
        top = jnp.maximum(top, codes[d])
    flags[0] = top
    spread = []
    for d in range(1, PLANE):
        copy = remote(
            flags.at[0], plane_flags.at[d], flag_send.at[d], flag_recv.at[d], hist=plane[d - 1]
        )
        copy.start()
        spread.append(copy)
    pass_on(moves[0])
    own_out(moves[1])
    for d in range(1, PLANE):
        spread[d - 1].wait_recv()
        top = jnp.maximum(top, plane_flags[d])
    flags[1] = top
    over = []
    for d in range(1, reps):
        copy = remote(
            flags.at[1], rep_flags.at[d], top_send.at[d], top_recv.at[d], rep=others[d - 1]
        )
        copy.start()
        over.append(copy)
    across(moves[0])
    for d in range(1, reps):
        over[d - 1].wait_recv()
        top = jnp.maximum(top, rep_flags[d])
    level_ref[0, 0] = top[0, 0]

    plane_ready(moves[0])
    for m in (0, 1, 2):
        moves[1][m].wait_recv()
    for group in [asks, spread, over, moves[0], moves[1][:3]]:
        for copy in group:
            copy.wait_send()


def ask(planes, reps, table, code):
    tiles, chunks, rows, width = table.shape
    dma = pltpu.SemaphoreType.DMA
    vmem = pl.BlockSpec(memory_space=pltpu.VMEM)
    words = pltpu.VMEM
    return pl.pallas_call(
        functools.partial(ask_kernel, planes, reps),
        out_shape=(
            jax.ShapeDtypeStruct((HELD, PLANE * tiles, rows, width), table.dtype),
            jax.ShapeDtypeStruct((planes, 1, 128), jnp.int32),
            jax.ShapeDtypeStruct((1, 1), jnp.int32),
        ),
        in_specs=[pl.BlockSpec(memory_space=pl.ANY), vmem],
        out_specs=(vmem, vmem, pl.BlockSpec(memory_space=pltpu.SMEM)),
        scratch_shapes=[
            words((2, 1, 128), jnp.int32),
            words((PLANE, 1, 128), jnp.int32),
            words((reps, 1, 128), jnp.int32),
            dma(()),
            dma((HELD,)),
            dma((planes,)),
            dma((planes,)),
            dma((PLANE,)),
            dma((PLANE,)),
            dma((reps,)),
            dma((reps,)),
            dma((HELD, 9)),
            dma((HELD, 9)),
        ],
        compiler_params=pltpu.CompilerParams(collective_id=0, has_side_effects=True, vmem_limit_bytes=16 << 20),
    )(table, code)


def gather_kernel(
    planes, far_room, near_room, table_ref, first_ref, codes, out_ref,
    tabs, stage_far, stage_near, far, near, far_end, near_end,
    load_sem, ring_send, ring_recv, far_send, far_recv, near_send, near_recv,
):
    me, z, y, c, hist = place(planes)
    sign = 1 - 2 * c
    half = planes // 2
    tiles = table_ref.shape[0]
    rows = table_ref.shape[2]
    slots = out_ref.shape[0]

    right, left, partner = hist(dy=1), hist(dy=-1), hist(dc=1)
    ahead, behind = hist(dz=sign), hist(dz=-sign)
    all_here = greet([{"hist": d} for d in (right, left, partner, ahead, behind)])
    most, one = pl.ds(0, 3 * tiles), pl.ds(4 * tiles, tiles)
    loads = [
        [pltpu.make_async_copy(first_ref.at[0], tabs[0], load_sem.at[0])],
        [
            pltpu.make_async_copy(first_ref.at[1, most], tabs[1].at[most], load_sem.at[1]),
            pltpu.make_async_copy(first_ref.at[1, one], tabs[1].at[one], load_sem.at[CHUNKS]),
        ],
    ] + [
        [
            pltpu.make_async_copy(
                table_ref.at[:, r], tabs[r].at[pl.ds(0, tiles)], load_sem.at[r]
            )
        ]
        for r in range(HELD, CHUNKS)
    ]
    for copies in loads:
        for copy in copies:
            copy.start()

    def loaded(r):
        for copy in loads[r]:
            copy.wait()

    moves = [[]]
    for r in range(1, CHUNKS):
        def link(which, src, dst, device, r=r):
            return remote(
                src, dst, ring_send.at[r, which], ring_recv.at[r, which], hist=device
            )

        moves.append(plane_moves(part_of(tabs[r], tiles), link, tiles, right, left, partner))

    def begin(r):
        loaded(r)
        own_out(moves[r])

    def second():
        loaded(1)
        pass_on(moves[1], False)

    def fill(r, dst, slot, lane, count, merge):
        def body(i, carry):
            code = codes[slot, 0, lane + i]
            tile = tabs[r][lax.rem(code, PLANE * tiles)]
            if merge:
                tile = jnp.where(lax.div(code, PLANE * tiles) == z, tile, dst[i])
            dst[i] = tile
            return carry

        lax.fori_loop(0, count, body, 0, unroll=2)

    def chain(stage, middle, end, room, send, recv, device):
        last = len(room) - 1
        ready = []
        for r in range(CHUNKS):
            hops = []
            for s, count in enumerate(room):
                src = stage.at[r] if s == 0 else middle.at[r, s - 1]
                dst = end[r] if s == last else middle.at[r, s]
                some = pl.ds(0, count)
                hops.append(
                    remote(src.at[some], dst.at[some], send.at[r, s], recv.at[r, s], hist=device)
                )
            ready.append(hops)
        return ready

    far_moves = chain(stage_far, far, far_end, far_room, far_send, far_recv, ahead)
    near_moves = chain(stage_near, near, near_end, near_room, near_send, near_recv, behind)

    def step(r, s):
        if s == 0:
            fill(r, stage_far.at[r], planes - half, FAR, far_room[0], False)
        else:
            far_moves[r][s - 1].wait_recv()
            fill(r, far.at[r, s - 1], planes - half + s, FAR, far_room[s], True)
        far_moves[r][s].start()
        if s < half - 1:
            distance = half - 1 - s
            if s == 0:
                fill(r, stage_near.at[r], distance, NEAR, near_room[0], False)
            else:
                near_moves[r][s - 1].wait_recv()
                fill(r, near.at[r, s - 1], distance, NEAR, near_room[s], True)
            near_moves[r][s].start()

    def finish(r):
        near_moves[r][half - 2].wait_recv()
        far_moves[r][half - 1].wait_recv()

        def body(i, carry):
            kind = codes[0, 0, KIND + i]
            spot = codes[0, 0, SPOT + i]
            tile = tabs[r][codes[0, 0, TILE + i]]
            other = jnp.where(kind == 1, far_end[r][spot], near_end[r][spot])
            out_ref[i, pl.ds(r * rows, rows)] = jnp.where(kind == 0, tile, other)
            return carry

        lax.fori_loop(0, slots, body, 0, unroll=2)

    events = [(-7, all_here, ()), (-5, second, ()), (-0.5, loaded, (0,))]
    for r in range(CHUNKS):
        if r >= HELD:
            events.append((half * r - BEGIN, begin, (r,)))
            events.append((half * r - PASS, pass_on, (moves[r],)))
        if r:
            events.append((half * r - ACROSS, across, (moves[r],)))
            events.append((half * r - 0.5, plane_ready, (moves[r], r >= HELD)))
        for s in range(half):
            events.append((half * r + STRIDE * s + 0.01 * r, step, (r, s)))
        events.append((half * r + STRIDE * half + 0.7, finish, (r,)))
    for _, act, args in sorted(events, key=lambda e: e[0]):
        act(*args)

    for group in [moves[1][3:]] + moves[HELD:] + far_moves + near_moves:
        for copy in group:
            copy.wait_send()


def pull(planes, level, far_room, near_room, table, first, codes):
    tiles, chunks, rows, width = table.shape
    slots = tiles
    half = planes // 2
    dma = pltpu.SemaphoreType.DMA
    block = (slots, rows, width)
    hbm = pl.BlockSpec(memory_space=pl.ANY)
    return pl.pallas_call(
        functools.partial(gather_kernel, planes, far_room, near_room),
        out_shape=jax.ShapeDtypeStruct((slots, chunks * rows, width), table.dtype),
        in_specs=[hbm, hbm, pl.BlockSpec(memory_space=pltpu.SMEM)],
        out_specs=pl.BlockSpec(memory_space=pltpu.VMEM),
        scratch_shapes=[
            [pltpu.VMEM((PLANE * tiles, rows, width), table.dtype)] * chunks,
            pltpu.VMEM((chunks,) + block, table.dtype),
            pltpu.VMEM((chunks,) + block, table.dtype),
            pltpu.VMEM((chunks, half - 1) + block, table.dtype),
            pltpu.VMEM((chunks, half - 2) + block, table.dtype),
            [pltpu.VMEM(block, table.dtype)] * chunks,
            [pltpu.VMEM(block, table.dtype)] * chunks,
            dma((chunks + 1,)),
            dma((chunks, 9)),
            dma((chunks, 9)),
            dma((chunks, half)),
            dma((chunks, half)),
            dma((chunks, half - 1)),
            dma((chunks, half - 1)),
        ],
        compiler_params=pltpu.CompilerParams(
            collective_id=2 + level, has_side_effects=True, vmem_limit_bytes=60 << 20
        ),
    )(table, first, codes)


def rooms(planes, slots):
    half = planes // 2
    full = ((slots,) * half, (slots,) * (half - 1))
    if (planes, slots) != (8, 16):
        return [full]
    return [
        ((6, 9, 11, 13), (6, 9, 11)),
        ((7, 10, 12, 14), (7, 10, 12)),
        ((9, 12, 14, 15), (9, 12, 14)),
        full,
    ]


def words_kernel(planes, levels, tiles, owner_ref, offset_ref, words, count, start):
    me, z, y, c, hist = place(planes)
    sign = 1 - 2 * c
    half = planes // 2
    slots = offset_ref.shape[1]

    def parse(k):
        owner = owner_ref[0, k]
        oz, oy, oc = position(owner)
        turn = lax.rem(oy - y + Y, Y)
        rel = jnp.where(turn == 0, 0, jnp.where(turn == 3, 1, jnp.where(turn == 1, 2, 3)))
        tile = (rel * CORES + jnp.abs(oc - c)) * tiles + offset_ref[0, k]
        away = lax.rem(sign * (z - oz) + planes, planes)
        return oz * (PLANE * tiles) + tile, tile, away

    any_code = parse(0)[0]
    for away in range(planes):
        count[away] = 0

    def tally(k, carry):
        away = parse(k)[2]
        count[away] += 1
        words[0, FAR + k] = any_code
        words[0, NEAR + k] = any_code
        return carry

    lax.fori_loop(0, slots, tally, 0)

    far_order = list(range(half, 0, -1))
    near_order = list(range(half + 1, planes))
    level = jnp.int32(0)
    start[0] = 0
    sums = []
    for order in (far_order, near_order):
        total = jnp.int32(0)
        ends = []
        for away in order:
            start[away] = total
            total = total + count[away]
            ends.append(total)
        sums.append(ends)
    for room in levels[:-1]:
        over = jnp.int32(0)
        for ends, caps in zip(sums, room):
            for end, cap in zip(ends, caps):
                over = jnp.maximum(over, jnp.where(end > cap, 1, 0))
        level = level + over
    words[0, LEVEL] = level

    def put(k, carry):
        code, tile, away = parse(k)
        spot = start[away]
        start[away] = spot + 1
        kind = jnp.where(away == 0, 0, jnp.where(away <= half, 1, 2))
        words[0, jnp.where(kind == 0, SPARE, jnp.where(kind == 1, FAR, NEAR)) + spot] = code
        words[0, KIND + k] = kind
        words[0, SPOT + k] = jnp.where(kind == 0, 0, spot)
        words[0, TILE + k] = tile
        return carry

    lax.fori_loop(0, slots, put, 0)


def requests(planes, levels, tiles, owners, offsets):
    smem = pl.BlockSpec(memory_space=pltpu.SMEM)
    return pl.pallas_call(
        functools.partial(words_kernel, planes, levels, tiles),
        out_shape=jax.ShapeDtypeStruct((1, 128), jnp.int32),
        in_specs=[smem, smem],
        out_specs=smem,
        scratch_shapes=[pltpu.SMEM((planes,), jnp.int32), pltpu.SMEM((planes,), jnp.int32)],
    )(owners, offsets)


GROUPS = 3
LAG = 1.1


def layer_kernel(
    planes, reps, relation_ref, pulled_ref, adjacency_ref, features_ref, cotangent_ref, weights_ref,
    fresh_ref, grad_x_ref, grad_w_ref,
    masked, stacked, pre_ref, dpre_ref, product, kept, give, take, y_bufs, x_bufs, y_sum, x_sum,
    x_out, x_in, y_out, y_in, mine, z_out, z_in, share,
    pair_send, pair_recv, y_send, y_recv, x_send, x_recv,
    x_put, x_get, y_put, y_get, z_send, z_recv, share_send, share_recv, weights_held, weights_sem,
):
    me, z, y, c, hist = place(planes)
    x = lax.axis_index("rep")
    blocks, tile, width = pulled_ref.shape
    mats = weights_ref.shape[0]
    relations = mats - 1
    batch_tiles = features_ref.shape[0] // tile
    per_tile = blocks // batch_tiles
    own_rows = width // (planes * PLANE)
    per = mats // GROUPS
    lanes = width // reps
    piece = planes * own_rows
    hp = piece // 2
    low, high = dpre_ref.dtype, jnp.float32

    right, left, partner = hist(dy=1), hist(dy=-1), hist(dc=1)
    column = [hist(dz=d) for d in range(1, planes)]
    ring = [hist(dy=d) for d in range(1, Y)]
    others = [lax.rem(x + d, reps) for d in range(1, reps)]
    all_here = greet(
        [{"hist": d} for d in column + ring + [partner]] + [{"rep": d} for d in others]
    )
    fetch = pltpu.make_async_copy(weights_ref, weights_held, weights_sem)
    fetch.start()

    stacked[0] = features_ref[...]
    pack = 2

    def mix(i, carry):
        t, q0 = lax.div(i, relations // pack), lax.rem(i, relations // pack) * pack
        for k in range(per_tile):
            relation = relation_ref[0, t * per_tile + k]
            block = adjacency_ref[t * per_tile + k]
            for p in range(pack):
                masked[p * tile:(p + 1) * tile, k * tile:(k + 1) * tile] = jnp.where(
                    relation == q0 + p, block, jnp.zeros_like(block)
                )
        rhs = pulled_ref[pl.ds(t * per_tile, per_tile)].reshape(per_tile * tile, width)
        total = jnp.dot(masked[...], rhs, preferred_element_type=high).astype(low)
        for p in range(pack):
            stacked[1 + q0 + p, pl.ds(t * tile, tile)] = total[p * tile:(p + 1) * tile]
        return carry

    lax.fori_loop(0, batch_tiles * relations // pack, mix, 0)

    fetch.wait()
    pre_ref[...] = jnp.dot(stacked[0], weights_held[0], preferred_element_type=high)

    def project(j, carry):
        pre_ref[...] += jnp.dot(stacked[j], weights_held[j], preferred_element_type=high)
        return carry

    lax.fori_loop(1, mats, project, 0)

    wide_x = features_ref[...].astype(high)
    wide_g = cotangent_ref[...].astype(high)
    pre = pre_ref[...]
    sigma = jax.nn.sigmoid(pre)
    fresh_ref[...] = (wide_x + pre * sigma).astype(fresh_ref.dtype)
    dpre_ref[...] = (wide_g * sigma * (1.0 + pre * (1.0 - sigma))).astype(low)

    pair = [
        remote(give.at[g], take.at[g], pair_send.at[g], pair_recv.at[g], hist=partner)
        for g in range(GROUPS)
    ]

    def products(g):
        def one(i, carry):
            value = lax.dot_general(
                stacked[g * per + i], dpre_ref[...], (((0,), (0,)), ((), ())),
                preferred_element_type=high,
            )
            product[...] = value.reshape(planes, Y, CORES, own_rows, width)
            for yy in range(Y):
                kept[g, yy, i] = product[:, yy, c].reshape(piece, width)
                give[g, yy, i] = product[:, yy, 1 - c].reshape(piece, width).astype(low)
            return carry

        lax.fori_loop(0, per, one, 0, unroll=True)
        pair[g].start()

    def y_part(g, yy, i):
        return kept[g, yy, i, :hp] + take[g, yy, i, :hp].astype(high)

    def x_part(g, xx, i):
        yy, j = lax.div(i, per), lax.rem(i, per)
        some = pl.ds(pl.multiple_of(xx * lanes, lanes), lanes)
        return kept[g, yy, j, hp:, some] + take[g, yy, j, hp:, some].astype(high)

    def around(size, axis, me_on, bufs, send, recv, part, count, result):
        far, to_next, to_prev, half_in, from_prev, from_next = bufs
        nxt, prv = lax.rem(me_on + 1, size), lax.rem(me_on + size - 1, size)
        across_it = lax.rem(me_on + 2, size)
        q = hp // 2
        top, bottom = pl.ds(0, q), pl.ds(q, q)
        to = (
            {"hist": right}, {"hist": left}
        ) if axis == "y" else ({"rep": nxt}, {"rep": prv})

        def turn(g, which, src, dst, device):
            return remote(src, dst, send.at[g, which], recv.at[g, which], **device)

        turns = [
            [
                turn(g, 0, far.at[g, :, top], half_in.at[g, :, top], to[0]),
                turn(g, 1, far.at[g, :, bottom], half_in.at[g, :, bottom], to[1]),
                turn(g, 2, to_next.at[g, :, bottom], from_prev.at[g, :, bottom], to[0]),
                turn(g, 3, to_prev.at[g, :, top], from_next.at[g, :, top], to[1]),
                turn(g, 4, to_next.at[g, :, top], from_prev.at[g, :, top], to[0]),
                turn(g, 5, to_prev.at[g, :, bottom], from_next.at[g, :, bottom], to[1]),
            ]
            for g in range(GROUPS)
        ]

        def first(g):
            def one(i, carry):
                far[g, i] = part(g, across_it, i).astype(low)
                to_next[g, i, bottom] = part(g, nxt, i)[q:].astype(low)
                to_prev[g, i, top] = part(g, prv, i)[:q].astype(low)
                return carry

            lax.fori_loop(0, count, one, 0)
            for m in range(4):
                turns[g][m].start()

        def second(g):
            turns[g][0].wait_recv()
            turns[g][1].wait_recv()

            def one(i, carry):
                up = part(g, nxt, i)[:q] + half_in[g, i, top].astype(high)
                down = part(g, prv, i)[q:] + half_in[g, i, bottom].astype(high)
                to_next[g, i, top] = up.astype(low)
                to_prev[g, i, bottom] = down.astype(low)
                return carry

            lax.fori_loop(0, count, one, 0)
            turns[g][4].start()
            turns[g][5].start()

        def last(g):
            for m in (2, 3, 4, 5):
                turns[g][m].wait_recv()

            def one(i, carry):
                result[g, i] = (
                    part(g, me_on, i)
                    + from_prev[g, i].astype(high)
                    + from_next[g, i].astype(high)
                )
                return carry

            lax.fori_loop(0, count, one, 0)

        return turns, first, second, last

    y_turns, y_first, y_second, y_last = around(
        Y, "y", y, y_bufs, y_send, y_recv, y_part, per, y_sum
    )
    x_turns, x_first, x_second, x_last = around(
        reps, "x", x, x_bufs, x_send, x_recv, x_part, Y * per, x_sum
    )

    def lanes_of(xx):
        return pl.ds(pl.multiple_of(xx * lanes, lanes), lanes)

    x_moves = [
        [
            remote(
                x_out.at[g, d], x_in.at[g, d], x_put.at[g, d], x_get.at[g, d], rep=others[d - 1]
            )
            for d in range(1, reps)
        ]
        for g in range(GROUPS)
    ]
    y_moves = [
        [
            remote(
                y_out.at[g, d], y_in.at[g, d], y_put.at[g, d], y_get.at[g, d], hist=ring[d - 1]
            )
            for d in range(1, Y)
        ]
        for g in range(GROUPS)
    ]

    def swap_x(g):
        for d in range(1, reps):
            x_out[g, d] = y_sum[g, :, :, lanes_of(others[d - 1])].astype(low)
            x_moves[g][d - 1].start()

    def swap_y(g):
        for d in range(1, Y):
            y_out[g, d] = x_sum[g, pl.ds(lax.rem(y + d, Y) * per, per)].astype(low)
            y_moves[g][d - 1].start()

    def join(g):
        total = y_sum[g, :, :, lanes_of(x)]
        for d in range(1, reps):
            x_moves[g][d - 1].wait_recv()
            total = total + x_in[g, d].astype(high)
        for i in range(per):
            mine[0:planes // 2, g, i] = total[i].reshape(planes // 2, own_rows, lanes)
        total = x_sum[g, pl.ds(y * per, per)]
        for d in range(1, Y):
            y_moves[g][d - 1].wait_recv()
            total = total + y_in[g, d].astype(high)
        for i in range(per):
            mine[planes // 2:, g, i] = total[i].reshape(planes // 2, own_rows, lanes)

    def first(g):
        pair[g].wait_recv()
        y_first(g)
        x_first(g)

    def second(g):
        y_second(g)
        x_second(g)

    def last(g):
        y_last(g)
        swap_x(g)
        x_last(g)
        swap_y(g)

    def extra():
        grad_x_ref[...] = (
            wide_g
            + lax.dot_general(
                dpre_ref[...], weights_held[0], (((1,), (1,)), ((), ())),
                preferred_element_type=high,
            )
        ).astype(grad_x_ref.dtype)

    all_here()
    z_rows = per * own_rows
    z_moves, share_moves = [], []
    for g in range(GROUPS):
        z_moves.append([
            remote(
                z_out.at[g, lax.rem(z + d, planes)], z_in.at[g, d],
                z_send.at[g, d], z_recv.at[g, d], hist=column[d - 1],
            )
            for d in range(1, planes)
        ])
        share_moves.append([
            remote(
                share.at[g, x], share.at[g, x], share_send.at[g, d], share_recv.at[g, d],
                rep=others[d - 1],
            )
            for d in range(1, reps)
        ])

    def up_down(g):
        def one(p, carry):
            rows = mine[p, g].reshape(z_rows, lanes)
            z_out[g, p, pl.ds(0, z_rows)] = rows.astype(low)
            return carry

        lax.fori_loop(0, planes, one, 0)
        for copy in z_moves[g]:
            copy.start()

    def gather_lanes(g):
        total = mine[z, g].reshape(z_rows, lanes)
        for d in range(1, planes):
            z_moves[g][d - 1].wait_recv()
            total = total + z_in[g, d, pl.ds(0, z_rows)].astype(high)
        share[g, x] = total
        for copy in share_moves[g]:
            copy.start()

    def hand_in(g):
        for copy in share_moves[g]:
            copy.wait_recv()
        for i in range(own_rows):
            for xx in range(reps):
                at = i * width + xx * lanes
                grad_w_ref[g * per:(g + 1) * per, at:at + lanes] = share[
                    g, xx, pl.ds(i, per, stride=own_rows)
                ]

    def collect(g):
        join(g)
        up_down(g)

    stages = [products, first, second, last, collect, gather_lanes, hand_in]
    extra_at = [(GROUPS - 0.5, -1, extra, ())]
    timed = [
        (g + LAG * lag, -lag, stage, (g,))
        for lag, stage in enumerate(stages)
        for g in range(GROUPS)
    ]
    for _, _, act, args in sorted(timed + extra_at, key=lambda e: e[:2]):
        act(*args)

    for group in [pair] + z_moves + share_moves + y_turns + x_turns + x_moves + y_moves:
        for copy in group:
            copy.wait_send()


def layer(planes, reps, relation, pulled, tiles, features, cotangent, weights):
    mats, width, _ = weights.shape
    batch = features.shape[0]
    blocks, tile, _ = pulled.shape
    per_tile = blocks * tile // batch
    own_rows = width // (planes * PLANE)
    per = mats // GROUPS
    piece = planes * own_rows
    hp = piece // 2
    lanes = width // reps
    z_pad = -(-per * own_rows // 16) * 16
    low, high = features.dtype, jnp.float32
    dma = pltpu.SemaphoreType.DMA
    vmem = pl.BlockSpec(memory_space=pltpu.VMEM)
    return pl.pallas_call(
        functools.partial(layer_kernel, planes, reps),
        out_shape=(
            jax.ShapeDtypeStruct((batch, width), low),
            jax.ShapeDtypeStruct((batch, width), low),
            jax.ShapeDtypeStruct((mats, own_rows * width), high),
        ),
        in_specs=[pl.BlockSpec(memory_space=pltpu.SMEM)] + [vmem] * 4 + [pl.BlockSpec(memory_space=pl.ANY)],
        out_specs=(vmem, vmem, vmem),
        scratch_shapes=[
            pltpu.VMEM((2 * tile, per_tile * tile), low),
            pltpu.VMEM((mats, batch, width), low),
            pltpu.VMEM((batch, width), high),
            pltpu.VMEM((batch, width), low),
            pltpu.VMEM((planes, Y, CORES, own_rows, width), high),
            pltpu.VMEM((GROUPS, Y, per, piece, width), high),
            pltpu.VMEM((GROUPS, Y, per, piece, width), low),
            pltpu.VMEM((GROUPS, Y, per, piece, width), low),
            [pltpu.VMEM((GROUPS, per, hp, width), low)] * 6,
            [pltpu.VMEM((GROUPS, Y * per, hp, lanes), low)] * 6,
            pltpu.VMEM((GROUPS, per, hp, width), high),
            pltpu.VMEM((GROUPS, Y * per, hp, lanes), high),
            pltpu.VMEM((GROUPS, reps, per, hp, lanes), low),
            pltpu.VMEM((GROUPS, reps, per, hp, lanes), low),
            pltpu.VMEM((GROUPS, Y, per, hp, lanes), low),
            pltpu.VMEM((GROUPS, Y, per, hp, lanes), low),
            pltpu.VMEM((planes, GROUPS, per, own_rows, lanes), high),
            pltpu.VMEM((GROUPS, planes, z_pad, lanes), low),
            pltpu.VMEM((GROUPS, planes, z_pad, lanes), low),
            pltpu.VMEM((GROUPS, reps, per * own_rows, lanes), high),
            dma((GROUPS,)),
            dma((GROUPS,)),
            dma((GROUPS, 6)),
            dma((GROUPS, 6)),
            dma((GROUPS, 6)),
            dma((GROUPS, 6)),
            dma((GROUPS, reps)),
            dma((GROUPS, reps)),
            dma((GROUPS, Y)),
            dma((GROUPS, Y)),
            dma((GROUPS, planes)),
            dma((GROUPS, planes)),
            dma((GROUPS, reps)),
            dma((GROUPS, reps)),
            pltpu.VMEM(weights.shape, low),
            dma(()),
        ],
        compiler_params=pltpu.CompilerParams(
            collective_id=1, has_side_effects=True, vmem_limit_bytes=60 << 20
        ),
    )(relation, pulled, tiles, features, cotangent, weights)


def hand_over_kernel(a_ref, b_ref, c_ref, a_out, b_out, c_out):
    a_out[...] = a_ref[...]
    b_out[...] = b_ref[...]
    c_out[...] = c_ref[...]


def hand_over(*results):
    vmem = pl.BlockSpec(memory_space=pltpu.VMEM)
    return pl.pallas_call(
        hand_over_kernel,
        out_shape=tuple(jax.ShapeDtypeStruct(r.shape, r.dtype) for r in results),
        in_specs=[vmem] * 3,
        out_specs=(vmem,) * 3,
    )(*results)


def on_device(
    planes, reps, features, history, blk_owner, blk_offset, blk_relation, adjacency, weights, cotangent
):
    tiles = adjacency[0]
    tile_rows = tiles.shape[-1]
    width = weights.shape[-1]
    mats = weights.shape[0]
    table = history.reshape(-1, tile_rows, width)

    tiles_held = table.shape[0]
    table = table.reshape(tiles_held, CHUNKS, tile_rows // CHUNKS, width)
    levels = rooms(planes, blk_offset.shape[1])
    words = requests(planes, levels, tiles_held, blk_owner.reshape(1, -1), blk_offset)
    first, codes, top = ask(planes, reps, table, words)
    pulled = lax.switch(
        top[0, 0],
        [
            functools.partial(pull, planes, level, far_room, near_room)
            for level, (far_room, near_room) in enumerate(levels)
        ],
        table, first, codes,
    )
    fresh, grad_x, grad_w = layer(
        planes, reps, blk_relation, pulled, tiles, features[0], cotangent[0], weights
    )
    fresh, grad_x, grad_w = hand_over(fresh, grad_x, grad_w)
    return fresh[None], grad_x[None], grad_w


def solution(mesh):
    planes = mesh.shape["hist"] // PLANE
    in_specs = (
        P("rep", "hist", None),
        P("rep", "hist", None),
        P("rep", "hist", None),
        P("rep", "hist"),
        P("rep", "hist"),
        P("rep", "hist", None, None),
        P(),
        P("rep", "hist", None),
    )
    out_specs = (P("rep", "hist", None), P("rep", "hist", None), P(None, "hist"))
    return jax.shard_map(
        functools.partial(on_device, planes, mesh.shape["rep"]),
        mesh=mesh, in_specs=in_specs, out_specs=out_specs, check_vma=False,
    )
```

```python
import functools

import jax
import jax.numpy as jnp
from jax import lax
from jax.experimental import pallas as pl
from jax.experimental.pallas import tpu as pltpu
from jax.sharding import PartitionSpec as P

Y = 4
CORES = 2
PLANE = Y * CORES
CHUNKS = 8
LEVEL, FAR, NEAR, KIND, SPOT, TILE, SPARE = 0, 16, 32, 48, 64, 80, 96
STRIDE = 3
HELD = 2
BEGIN, PASS, ACROSS = 7.3, 3.5, 1.5


def position(index):
    return lax.div(index, PLANE), lax.rem(lax.div(index, CORES), Y), lax.rem(index, CORES)


def place(plane_count):
    me = lax.axis_index("hist")
    z, y, c = position(me)

    def hist(dz=0, dy=0, dc=0):
        zz = lax.rem(z + dz + plane_count, plane_count)
        yy = lax.rem(y + dy + Y, Y)
        cc = lax.rem(c + dc, CORES)
        return (zz * Y + yy) * CORES + cc

    return me, z, y, c, hist


def remote(src, dst, send, recv, **device):
    return pltpu.make_async_remote_copy(
        src_ref=src,
        dst_ref=dst,
        send_sem=send,
        recv_sem=recv,
        device_id=device,
        device_id_type=pl.DeviceIdType.MESH,
    )


def greet(partners):
    barrier = pltpu.get_barrier_semaphore()
    for device in partners:
        pl.semaphore_signal(
            barrier, inc=1, device_id=device, device_id_type=pl.DeviceIdType.MESH
        )
    return lambda: pl.semaphore_wait(barrier, len(partners))


def plane_moves(part, link, tiles, right, left, partner):
    h = tiles // 2
    return [
        link(0, part(0, 0), part(1, 0), right),
        link(1, part(0, 0), part(2, 0), left),
        link(2, part(0, 0), part(0, 1), partner),
        link(3, part(1, 0, 0, h), part(3, 0, 0, h), right),
        link(4, part(2, 0, h, h), part(3, 0, h, h), left),
        link(5, part(1, 0), part(1, 1), partner),
        link(6, part(2, 0), part(2, 1), partner),
        link(7, part(3, 0, 0, h), part(3, 1, 0, h), partner),
        link(8, part(3, 0, h, h), part(3, 1, h, h), partner),
    ]


def own_out(moves):
    for m in (0, 1, 2):
        moves[m].start()


def pass_on(moves, wait=True):
    if wait:
        moves[0].wait_recv()
    moves[3].start()
    if wait:
        moves[1].wait_recv()
    moves[4].start()
    moves[5].start()
    moves[6].start()


def across(moves):
    moves[3].wait_recv()
    moves[7].start()
    moves[4].wait_recv()
    moves[8].start()


def plane_ready(moves, own=True):
    for m in (2, 5, 6, 7, 8) if own else (5, 6, 7, 8):
        moves[m].wait_recv()


def part_of(ref, tiles):
    def part(rel, core, lo=0, n=tiles):
        return ref.at[pl.ds((rel * CORES + core) * tiles + lo, n)]

    return part


def ask_kernel(
    planes, reps, table_ref, code_ref, tab_ref, codes, level_ref,
    flags, plane_flags, rep_flags, own_sem, load_sem, code_send, code_recv,
    flag_send, flag_recv, top_send, top_recv, ring_send, ring_recv,
):
    me, z, y, c, hist = place(planes)
    sign = 1 - 2 * c
    x = lax.axis_index("rep")
    tiles = table_ref.shape[0]
    right, left, partner = hist(dy=1), hist(dy=-1), hist(dc=1)
    column = [hist(dz=sign * d) for d in range(1, planes)]
    plane = [hist(dy=d // CORES, dc=d % CORES) for d in range(1, PLANE)]
    others = [lax.rem(x + d, reps) for d in range(1, reps)]
    all_here = greet(
        [{"hist": d} for d in column + plane] + [{"rep": d} for d in others]
    )
    parts = [part_of(tab_ref.at[r], tiles) for r in range(HELD)]
    loads = [
        pltpu.make_async_copy(table_ref.at[:, r], parts[r](0, 0), load_sem.at[r])
        for r in range(HELD)
    ]
    for copy in loads:
        copy.start()
    all_here()

    own = pltpu.make_async_copy(code_ref, codes.at[0], own_sem)
    own.start()
    asks = []
    for d in range(1, planes):
        copy = remote(
            code_ref, codes.at[d], code_send.at[d], code_recv.at[d], hist=column[d - 1]
        )
        copy.start()
        asks.append(copy)

    moves = []
    for r in range(HELD):
        def link(which, src, dst, device, r=r):
            return remote(
                src, dst, ring_send.at[r, which], ring_recv.at[r, which], hist=device
            )

        moves.append(plane_moves(parts[r], link, tiles, right, left, partner))
        loads[r].wait()
        if r == 0:
            own_out(moves[0])

    own.wait()
    for copy in asks:
        copy.wait_recv()
    top = codes[0]
    for d in range(1, planes):
        top = jnp.maximum(top, codes[d])
    flags[0] = top
    spread = []
    for d in range(1, PLANE):
        copy = remote(
            flags.at[0], plane_flags.at[d], flag_send.at[d], flag_recv.at[d], hist=plane[d - 1]
        )
        copy.start()
        spread.append(copy)
    pass_on(moves[0])
    own_out(moves[1])
    for d in range(1, PLANE):
        spread[d - 1].wait_recv()
        top = jnp.maximum(top, plane_flags[d])
    flags[1] = top
    over = []
    for d in range(1, reps):
        copy = remote(
            flags.at[1], rep_flags.at[d], top_send.at[d], top_recv.at[d], rep=others[d - 1]
        )
        copy.start()
        over.append(copy)
    across(moves[0])
    for d in range(1, reps):
        over[d - 1].wait_recv()
        top = jnp.maximum(top, rep_flags[d])
    level_ref[0, 0] = top[0, 0]

    plane_ready(moves[0])
    for m in (0, 1, 2):
        moves[1][m].wait_recv()
    for group in [asks, spread, over, moves[0], moves[1][:3]]:
        for copy in group:
            copy.wait_send()


def ask(planes, reps, table, code):
    tiles, chunks, rows, width = table.shape
    dma = pltpu.SemaphoreType.DMA
    vmem = pl.BlockSpec(memory_space=pltpu.VMEM)
    words = pltpu.VMEM
    return pl.pallas_call(
        functools.partial(ask_kernel, planes, reps),
        out_shape=(
            jax.ShapeDtypeStruct((HELD, PLANE * tiles, rows, width), table.dtype),
            jax.ShapeDtypeStruct((planes, 1, 128), jnp.int32),
            jax.ShapeDtypeStruct((1, 1), jnp.int32),
        ),
        in_specs=[pl.BlockSpec(memory_space=pl.ANY), vmem],
        out_specs=(vmem, vmem, pl.BlockSpec(memory_space=pltpu.SMEM)),
        scratch_shapes=[
            words((2, 1, 128), jnp.int32),
            words((PLANE, 1, 128), jnp.int32),
            words((reps, 1, 128), jnp.int32),
            dma(()),
            dma((HELD,)),
            dma((planes,)),
            dma((planes,)),
            dma((PLANE,)),
            dma((PLANE,)),
            dma((reps,)),
            dma((reps,)),
            dma((HELD, 9)),
            dma((HELD, 9)),
        ],
        compiler_params=pltpu.CompilerParams(collective_id=0, has_side_effects=True, vmem_limit_bytes=16 << 20),
    )(table, code)


def gather_kernel(
    planes, far_room, near_room, table_ref, first_ref, codes, out_ref,
    tabs, stage_far, stage_near, far, near, far_end, near_end,
    load_sem, ring_send, ring_recv, far_send, far_recv, near_send, near_recv,
):
    me, z, y, c, hist = place(planes)
    sign = 1 - 2 * c
    half = planes // 2
    tiles = table_ref.shape[0]
    rows = table_ref.shape[2]
    slots = out_ref.shape[0]

    right, left, partner = hist(dy=1), hist(dy=-1), hist(dc=1)
    ahead, behind = hist(dz=sign), hist(dz=-sign)
    all_here = greet([{"hist": d} for d in (right, left, partner, ahead, behind)])
    most, one = pl.ds(0, 3 * tiles), pl.ds(4 * tiles, tiles)
    loads = [
        [pltpu.make_async_copy(first_ref.at[0], tabs[0], load_sem.at[0])],
        [
            pltpu.make_async_copy(first_ref.at[1, most], tabs[1].at[most], load_sem.at[1]),
            pltpu.make_async_copy(first_ref.at[1, one], tabs[1].at[one], load_sem.at[CHUNKS]),
        ],
    ] + [
        [
            pltpu.make_async_copy(
                table_ref.at[:, r], tabs[r].at[pl.ds(0, tiles)], load_sem.at[r]
            )
        ]
        for r in range(HELD, CHUNKS)
    ]
    for copies in loads:
        for copy in copies:
            copy.start()

    def loaded(r):
        for copy in loads[r]:
            copy.wait()

    moves = [[]]
    for r in range(1, CHUNKS):
        def link(which, src, dst, device, r=r):
            return remote(
                src, dst, ring_send.at[r, which], ring_recv.at[r, which], hist=device
            )

        moves.append(plane_moves(part_of(tabs[r], tiles), link, tiles, right, left, partner))

    def begin(r):
        loaded(r)
        own_out(moves[r])

    def second():
        loaded(1)
        pass_on(moves[1], False)

    def fill(r, dst, slot, lane, count, merge):
        def body(i, carry):
            code = codes[slot, 0, lane + i]
            tile = tabs[r][lax.rem(code, PLANE * tiles)]
            if merge:
                tile = jnp.where(lax.div(code, PLANE * tiles) == z, tile, dst[i])
            dst[i] = tile
            return carry

        lax.fori_loop(0, count, body, 0, unroll=2)

    def chain(stage, middle, end, room, send, recv, device):
        last = len(room) - 1
        ready = []
        for r in range(CHUNKS):
            hops = []
            for s, count in enumerate(room):
                src = stage.at[r] if s == 0 else middle.at[r, s - 1]
                dst = end[r] if s == last else middle.at[r, s]
                some = pl.ds(0, count)
                hops.append(
                    remote(src.at[some], dst.at[some], send.at[r, s], recv.at[r, s], hist=device)
                )
            ready.append(hops)
        return ready

    far_moves = chain(stage_far, far, far_end, far_room, far_send, far_recv, ahead)
    near_moves = chain(stage_near, near, near_end, near_room, near_send, near_recv, behind)

    def step(r, s):
        if s == 0:
            fill(r, stage_far.at[r], planes - half, FAR, far_room[0], False)
        else:
            far_moves[r][s - 1].wait_recv()
            fill(r, far.at[r, s - 1], planes - half + s, FAR, far_room[s], True)
        far_moves[r][s].start()
        if s < half - 1:
            distance = half - 1 - s
            if s == 0:
                fill(r, stage_near.at[r], distance, NEAR, near_room[0], False)
            else:
                near_moves[r][s - 1].wait_recv()
                fill(r, near.at[r, s - 1], distance, NEAR, near_room[s], True)
            near_moves[r][s].start()

    def finish(r):
        near_moves[r][half - 2].wait_recv()
        far_moves[r][half - 1].wait_recv()

        def body(i, carry):
            kind = codes[0, 0, KIND + i]
            spot = codes[0, 0, SPOT + i]
            tile = tabs[r][codes[0, 0, TILE + i]]
            other = jnp.where(kind == 1, far_end[r][spot], near_end[r][spot])
            out_ref[i, pl.ds(r * rows, rows)] = jnp.where(kind == 0, tile, other)
            return carry

        lax.fori_loop(0, slots, body, 0, unroll=2)

    events = [(-7, all_here, ()), (-5, second, ()), (-0.5, loaded, (0,))]
    for r in range(CHUNKS):
        if r >= HELD:
            events.append((half * r - BEGIN, begin, (r,)))
            events.append((half * r - PASS, pass_on, (moves[r],)))
        if r:
            events.append((half * r - ACROSS, across, (moves[r],)))
            events.append((half * r - 0.5, plane_ready, (moves[r], r >= HELD)))
        for s in range(half):
            events.append((half * r + STRIDE * s + 0.01 * r, step, (r, s)))
        events.append((half * r + STRIDE * half + 0.7, finish, (r,)))
    for _, act, args in sorted(events, key=lambda e: e[0]):
        act(*args)

    for group in [moves[1][3:]] + moves[HELD:] + far_moves + near_moves:
        for copy in group:
            copy.wait_send()


def pull(planes, level, far_room, near_room, table, first, codes):
    tiles, chunks, rows, width = table.shape
    slots = tiles
    half = planes // 2
    dma = pltpu.SemaphoreType.DMA
    block = (slots, rows, width)
    hbm = pl.BlockSpec(memory_space=pl.ANY)
    return pl.pallas_call(
        functools.partial(gather_kernel, planes, far_room, near_room),
        out_shape=jax.ShapeDtypeStruct((slots, chunks * rows, width), table.dtype),
        in_specs=[hbm, hbm, pl.BlockSpec(memory_space=pltpu.SMEM)],
        out_specs=pl.BlockSpec(memory_space=pltpu.VMEM),
        scratch_shapes=[
            [pltpu.VMEM((PLANE * tiles, rows, width), table.dtype)] * chunks,
            pltpu.VMEM((chunks,) + block, table.dtype),
            pltpu.VMEM((chunks,) + block, table.dtype),
            pltpu.VMEM((chunks, half - 1) + block, table.dtype),
            pltpu.VMEM((chunks, half - 2) + block, table.dtype),
            [pltpu.VMEM(block, table.dtype)] * chunks,
            [pltpu.VMEM(block, table.dtype)] * chunks,
            dma((chunks + 1,)),
            dma((chunks, 9)),
            dma((chunks, 9)),
            dma((chunks, half)),
            dma((chunks, half)),
            dma((chunks, half - 1)),
            dma((chunks, half - 1)),
        ],
        compiler_params=pltpu.CompilerParams(
            collective_id=2 + level, has_side_effects=True, vmem_limit_bytes=60 << 20
        ),
    )(table, first, codes)


def rooms(planes, slots):
    half = planes // 2
    full = ((slots,) * half, (slots,) * (half - 1))
    if (planes, slots) != (8, 16):
        return [full]
    return [
        ((6, 9, 11, 13), (6, 9, 11)),
        ((7, 10, 12, 14), (7, 10, 12)),
        ((9, 12, 14, 15), (9, 12, 14)),
        full,
    ]


def words_kernel(planes, levels, tiles, owner_ref, offset_ref, words, count, start):
    me, z, y, c, hist = place(planes)
    sign = 1 - 2 * c
    half = planes // 2
    slots = offset_ref.shape[1]

    def parse(k):
        owner = owner_ref[0, k]
        oz, oy, oc = position(owner)
        turn = lax.rem(oy - y + Y, Y)
        rel = jnp.where(turn == 0, 0, jnp.where(turn == 3, 1, jnp.where(turn == 1, 2, 3)))
        tile = (rel * CORES + jnp.abs(oc - c)) * tiles + offset_ref[0, k]
        away = lax.rem(sign * (z - oz) + planes, planes)
        return oz * (PLANE * tiles) + tile, tile, away

    any_code = parse(0)[0]
    for away in range(planes):
        count[away] = 0

    def tally(k, carry):
        away = parse(k)[2]
        count[away] += 1
        words[0, FAR + k] = any_code
        words[0, NEAR + k] = any_code
        return carry

    lax.fori_loop(0, slots, tally, 0)

    far_order = list(range(half, 0, -1))
    near_order = list(range(half + 1, planes))
    level = jnp.int32(0)
    start[0] = 0
    sums = []
    for order in (far_order, near_order):
        total = jnp.int32(0)
        ends = []
        for away in order:
            start[away] = total
            total = total + count[away]
            ends.append(total)
        sums.append(ends)
    for room in levels[:-1]:
        over = jnp.int32(0)
        for ends, caps in zip(sums, room):
            for end, cap in zip(ends, caps):
                over = jnp.maximum(over, jnp.where(end > cap, 1, 0))
        level = level + over
    words[0, LEVEL] = level

    def put(k, carry):
        code, tile, away = parse(k)
        spot = start[away]
        start[away] = spot + 1
        kind = jnp.where(away == 0, 0, jnp.where(away <= half, 1, 2))
        words[0, jnp.where(kind == 0, SPARE, jnp.where(kind == 1, FAR, NEAR)) + spot] = code
        words[0, KIND + k] = kind
        words[0, SPOT + k] = jnp.where(kind == 0, 0, spot)
        words[0, TILE + k] = tile
        return carry

    lax.fori_loop(0, slots, put, 0)


def requests(planes, levels, tiles, owners, offsets):
    smem = pl.BlockSpec(memory_space=pltpu.SMEM)
    return pl.pallas_call(
        functools.partial(words_kernel, planes, levels, tiles),
        out_shape=jax.ShapeDtypeStruct((1, 128), jnp.int32),
        in_specs=[smem, smem],
        out_specs=smem,
        scratch_shapes=[pltpu.SMEM((planes,), jnp.int32), pltpu.SMEM((planes,), jnp.int32)],
    )(owners, offsets)


GROUPS = 3
LAG = 1.1


def layer_kernel(
    planes, reps, relation_ref, pulled_ref, adjacency_ref, features_ref, cotangent_ref, weights_ref,
    fresh_ref, grad_x_ref, grad_w_ref,
    masked, stacked, pre_ref, dpre_ref, product, kept, give, take, y_bufs, x_bufs, y_sum, x_sum,
    x_out, x_in, y_out, y_in, mine, z_out, z_in, share,
    pair_send, pair_recv, y_send, y_recv, x_send, x_recv,
    x_put, x_get, y_put, y_get, z_send, z_recv, share_send, share_recv, weights_held, weights_sem,
):
    me, z, y, c, hist = place(planes)
    x = lax.axis_index("rep")
    blocks, tile, width = pulled_ref.shape
    mats = weights_ref.shape[0]
    relations = mats - 1
    batch_tiles = features_ref.shape[0] // tile
    per_tile = blocks // batch_tiles
    own_rows = width // (planes * PLANE)
    per = mats // GROUPS
    lanes = width // reps
    piece = planes * own_rows
    hp = piece // 2
    low, high = dpre_ref.dtype, jnp.float32

    right, left, partner = hist(dy=1), hist(dy=-1), hist(dc=1)
    column = [hist(dz=d) for d in range(1, planes)]
    ring = [hist(dy=d) for d in range(1, Y)]
    others = [lax.rem(x + d, reps) for d in range(1, reps)]
    all_here = greet(
        [{"hist": d} for d in column + ring + [partner]] + [{"rep": d} for d in others]
    )
    fetch = pltpu.make_async_copy(weights_ref, weights_held, weights_sem)
    fetch.start()

    stacked[0] = features_ref[...]
    pack = 2

    def mix(i, carry):
        t, q0 = lax.div(i, relations // pack), lax.rem(i, relations // pack) * pack
        for k in range(per_tile):
            relation = relation_ref[0, t * per_tile + k]
            block = adjacency_ref[t * per_tile + k]
            for p in range(pack):
                masked[p * tile:(p + 1) * tile, k * tile:(k + 1) * tile] = jnp.where(
                    relation == q0 + p, block, jnp.zeros_like(block)
                )
        rhs = pulled_ref[pl.ds(t * per_tile, per_tile)].reshape(per_tile * tile, width)
        total = jnp.dot(masked[...], rhs, preferred_element_type=high).astype(low)
        for p in range(pack):
            stacked[1 + q0 + p, pl.ds(t * tile, tile)] = total[p * tile:(p + 1) * tile]
        return carry

    lax.fori_loop(0, batch_tiles * relations // pack, mix, 0)

    fetch.wait()
    pre_ref[...] = jnp.dot(stacked[0], weights_held[0], preferred_element_type=high)

    def project(j, carry):
        pre_ref[...] += jnp.dot(stacked[j], weights_held[j], preferred_element_type=high)
        return carry

    lax.fori_loop(1, mats, project, 0)

    wide_x = features_ref[...].astype(high)
    wide_g = cotangent_ref[...].astype(high)
    pre = pre_ref[...]
    sigma = jax.nn.sigmoid(pre)
    fresh_ref[...] = (wide_x + pre * sigma).astype(fresh_ref.dtype)
    dpre_ref[...] = (wide_g * sigma * (1.0 + pre * (1.0 - sigma))).astype(low)

    pair = [
        remote(give.at[g], take.at[g], pair_send.at[g], pair_recv.at[g], hist=partner)
        for g in range(GROUPS)
    ]

    def products(g):
        def one(i, carry):
            value = lax.dot_general(
                stacked[g * per + i], dpre_ref[...], (((0,), (0,)), ((), ())),
                preferred_element_type=high,
            )
            product[...] = value.reshape(planes, Y, CORES, own_rows, width)
            for yy in range(Y):
                kept[g, yy, i] = product[:, yy, c].reshape(piece, width)
                give[g, yy, i] = product[:, yy, 1 - c].reshape(piece, width).astype(give.dtype)
            return carry

        lax.fori_loop(0, per, one, 0, unroll=True)
        pair[g].start()

    def y_part(g, yy, i):
        return kept[g, yy, i, :hp] + take[g, yy, i, :hp].astype(high)

    def x_part(g, xx, i):
        yy, j = lax.div(i, per), lax.rem(i, per)
        some = pl.ds(pl.multiple_of(xx * lanes, lanes), lanes)
        return kept[g, yy, j, hp:, some] + take[g, yy, j, hp:, some].astype(high)

    def around(size, axis, me_on, bufs, send, recv, part, count, result):
        far, to_next, to_prev, half_in, from_prev, from_next = bufs
        nxt, prv = lax.rem(me_on + 1, size), lax.rem(me_on + size - 1, size)
        across_it = lax.rem(me_on + 2, size)
        q = hp // 2
        top, bottom = pl.ds(0, q), pl.ds(q, q)
        to = (
            {"hist": right}, {"hist": left}
        ) if axis == "y" else ({"rep": nxt}, {"rep": prv})

        def turn(g, which, src, dst, device):
            return remote(src, dst, send.at[g, which], recv.at[g, which], **device)

        turns = [
            [
                turn(g, 0, far.at[g, :, top], half_in.at[g, :, top], to[0]),
                turn(g, 1, far.at[g, :, bottom], half_in.at[g, :, bottom], to[1]),
                turn(g, 2, to_next.at[g, :, bottom], from_prev.at[g, :, bottom], to[0]),
                turn(g, 3, to_prev.at[g, :, top], from_next.at[g, :, top], to[1]),
                turn(g, 4, to_next.at[g, :, top], from_prev.at[g, :, top], to[0]),
                turn(g, 5, to_prev.at[g, :, bottom], from_next.at[g, :, bottom], to[1]),
            ]
            for g in range(GROUPS)
        ]

        def first(g):
            def one(i, carry):
                far[g, i] = part(g, across_it, i).astype(far.dtype)
                to_next[g, i, bottom] = part(g, nxt, i)[q:].astype(far.dtype)
                to_prev[g, i, top] = part(g, prv, i)[:q].astype(far.dtype)
                return carry

            lax.fori_loop(0, count, one, 0)
            for m in range(4):
                turns[g][m].start()

        def second(g):
            turns[g][0].wait_recv()
            turns[g][1].wait_recv()

            def one(i, carry):
                up = part(g, nxt, i)[:q] + half_in[g, i, top].astype(high)
                down = part(g, prv, i)[q:] + half_in[g, i, bottom].astype(high)
                to_next[g, i, top] = up.astype(far.dtype)
                to_prev[g, i, bottom] = down.astype(far.dtype)
                return carry

            lax.fori_loop(0, count, one, 0)
            turns[g][4].start()
            turns[g][5].start()

        def last(g):
            for m in (2, 3, 4, 5):
                turns[g][m].wait_recv()

            def one(i, carry):
                result[g, i] = (
                    part(g, me_on, i)
                    + from_prev[g, i].astype(high)
                    + from_next[g, i].astype(high)
                )
                return carry

            lax.fori_loop(0, count, one, 0)

        return turns, first, second, last

    y_turns, y_first, y_second, y_last = around(
        Y, "y", y, y_bufs, y_send, y_recv, y_part, per, y_sum
    )
    x_turns, x_first, x_second, x_last = around(
        reps, "x", x, x_bufs, x_send, x_recv, x_part, Y * per, x_sum
    )

    def lanes_of(xx):
        return pl.ds(pl.multiple_of(xx * lanes, lanes), lanes)

    x_moves = [
        [
            remote(
                x_out.at[g, d], x_in.at[g, d], x_put.at[g, d], x_get.at[g, d], rep=others[d - 1]
            )
            for d in range(1, reps)
        ]
        for g in range(GROUPS)
    ]
    y_moves = [
        [
            remote(
                y_out.at[g, d], y_in.at[g, d], y_put.at[g, d], y_get.at[g, d], hist=ring[d - 1]
            )
            for d in range(1, Y)
        ]
        for g in range(GROUPS)
    ]

    def swap_x(g):
        for d in range(1, reps):
            x_out[g, d] = y_sum[g, :, :, lanes_of(others[d - 1])].astype(x_out.dtype)
            x_moves[g][d - 1].start()

    def swap_y(g):
        for d in range(1, Y):
            y_out[g, d] = x_sum[g, pl.ds(lax.rem(y + d, Y) * per, per)].astype(y_out.dtype)
            y_moves[g][d - 1].start()

    def join(g):
        total = y_sum[g, :, :, lanes_of(x)]
        for d in range(1, reps):
            x_moves[g][d - 1].wait_recv()
            total = total + x_in[g, d].astype(high)
        for i in range(per):
            mine[0:planes // 2, g, i] = total[i].reshape(planes // 2, own_rows, lanes)
        total = x_sum[g, pl.ds(y * per, per)]
        for d in range(1, Y):
            y_moves[g][d - 1].wait_recv()
            total = total + y_in[g, d].astype(high)
        for i in range(per):
            mine[planes // 2:, g, i] = total[i].reshape(planes // 2, own_rows, lanes)

    def first(g):
        pair[g].wait_recv()
        y_first(g)
        x_first(g)

    def second(g):
        y_second(g)
        x_second(g)

    def last(g):
        y_last(g)
        swap_x(g)
        x_last(g)
        swap_y(g)

    def extra():
        grad_x_ref[...] = (
            wide_g
            + lax.dot_general(
                dpre_ref[...], weights_held[0], (((1,), (1,)), ((), ())),
                preferred_element_type=high,
            )
        ).astype(grad_x_ref.dtype)

    all_here()
    z_rows = per * own_rows
    z_moves, share_moves = [], []
    for g in range(GROUPS):
        z_moves.append([
            remote(
                z_out.at[g, lax.rem(z + d, planes)], z_in.at[g, d],
                z_send.at[g, d], z_recv.at[g, d], hist=column[d - 1],
            )
            for d in range(1, planes)
        ])
        share_moves.append([
            remote(
                share.at[g, x], share.at[g, x], share_send.at[g, d], share_recv.at[g, d],
                rep=others[d - 1],
            )
            for d in range(1, reps)
        ])

    def up_down(g):
        def one(p, carry):
            rows = mine[p, g].reshape(z_rows, lanes)
            z_out[g, p, pl.ds(0, z_rows)] = rows.astype(z_out.dtype)
            return carry

        lax.fori_loop(0, planes, one, 0)
        for copy in z_moves[g]:
            copy.start()

    def gather_lanes(g):
        total = mine[z, g].reshape(z_rows, lanes)
        for d in range(1, planes):
            z_moves[g][d - 1].wait_recv()
            total = total + z_in[g, d, pl.ds(0, z_rows)].astype(high)
        share[g, x] = total
        for copy in share_moves[g]:
            copy.start()

    def hand_in(g):
        for copy in share_moves[g]:
            copy.wait_recv()
        for i in range(own_rows):
            for xx in range(reps):
                at = i * width + xx * lanes
                grad_w_ref[g * per:(g + 1) * per, at:at + lanes] = share[
                    g, xx, pl.ds(i, per, stride=own_rows)
                ]

    def collect(g):
        join(g)
        up_down(g)

    stages = [products, first, second, last, collect, gather_lanes, hand_in]
    extra_at = [(GROUPS - 0.5, -1, extra, ())]
    timed = [
        (g + LAG * lag, -lag, stage, (g,))
        for lag, stage in enumerate(stages)
        for g in range(GROUPS)
    ]
    for _, _, act, args in sorted(timed + extra_at, key=lambda e: e[:2]):
        act(*args)

    for group in [pair] + z_moves + share_moves + y_turns + x_turns + x_moves + y_moves:
        for copy in group:
            copy.wait_send()


def layer(planes, reps, relation, pulled, tiles, features, cotangent, weights):
    mats, width, _ = weights.shape
    batch = features.shape[0]
    blocks, tile, _ = pulled.shape
    per_tile = blocks * tile // batch
    own_rows = width // (planes * PLANE)
    per = mats // GROUPS
    piece = planes * own_rows
    hp = piece // 2
    lanes = width // reps
    z_pad = -(-per * own_rows // 16) * 16
    low, high = features.dtype, jnp.float32
    dma = pltpu.SemaphoreType.DMA
    vmem = pl.BlockSpec(memory_space=pltpu.VMEM)
    return pl.pallas_call(
        functools.partial(layer_kernel, planes, reps),
        out_shape=(
            jax.ShapeDtypeStruct((batch, width), low),
            jax.ShapeDtypeStruct((batch, width), low),
            jax.ShapeDtypeStruct((mats, own_rows * width), high),
        ),
        in_specs=[pl.BlockSpec(memory_space=pltpu.SMEM)] + [vmem] * 4 + [pl.BlockSpec(memory_space=pl.ANY)],
        out_specs=(vmem, vmem, vmem),
        scratch_shapes=[
            pltpu.VMEM((2 * tile, per_tile * tile), low),
            pltpu.VMEM((mats, batch, width), low),
            pltpu.VMEM((batch, width), high),
            pltpu.VMEM((batch, width), low),
            pltpu.VMEM((planes, Y, CORES, own_rows, width), high),
            pltpu.VMEM((GROUPS, Y, per, piece, width), high),
            pltpu.VMEM((GROUPS, Y, per, piece, width), high),
            pltpu.VMEM((GROUPS, Y, per, piece, width), high),
            [pltpu.VMEM((GROUPS, per, hp, width), high)] * 6,
            [pltpu.VMEM((GROUPS, Y * per, hp, lanes), high)] * 6,
            pltpu.VMEM((GROUPS, per, hp, width), high),
            pltpu.VMEM((GROUPS, Y * per, hp, lanes), high),
            pltpu.VMEM((GROUPS, reps, per, hp, lanes), high),
            pltpu.VMEM((GROUPS, reps, per, hp, lanes), high),
            pltpu.VMEM((GROUPS, Y, per, hp, lanes), high),
            pltpu.VMEM((GROUPS, Y, per, hp, lanes), high),
            pltpu.VMEM((planes, GROUPS, per, own_rows, lanes), high),
            pltpu.VMEM((GROUPS, planes, z_pad, lanes), high),
            pltpu.VMEM((GROUPS, planes, z_pad, lanes), high),
            pltpu.VMEM((GROUPS, reps, per * own_rows, lanes), high),
            dma((GROUPS,)),
            dma((GROUPS,)),
            dma((GROUPS, 6)),
            dma((GROUPS, 6)),
            dma((GROUPS, 6)),
            dma((GROUPS, 6)),
            dma((GROUPS, reps)),
            dma((GROUPS, reps)),
            dma((GROUPS, Y)),
            dma((GROUPS, Y)),
            dma((GROUPS, planes)),
            dma((GROUPS, planes)),
            dma((GROUPS, reps)),
            dma((GROUPS, reps)),
            pltpu.VMEM(weights.shape, low),
            dma(()),
        ],
        compiler_params=pltpu.CompilerParams(
            collective_id=1, has_side_effects=True, vmem_limit_bytes=60 << 20
        ),
    )(relation, pulled, tiles, features, cotangent, weights)


def hand_over_kernel(a_ref, b_ref, c_ref, a_out, b_out, c_out):
    a_out[...] = a_ref[...]
    b_out[...] = b_ref[...]
    c_out[...] = c_ref[...]


def hand_over(*results):
    vmem = pl.BlockSpec(memory_space=pltpu.VMEM)
    return pl.pallas_call(
        hand_over_kernel,
        out_shape=tuple(jax.ShapeDtypeStruct(r.shape, r.dtype) for r in results),
        in_specs=[vmem] * 3,
        out_specs=(vmem,) * 3,
    )(*results)


def on_device(
    planes, reps, features, history, blk_owner, blk_offset, blk_relation, adjacency, weights, cotangent
):
    tiles = adjacency[0]
    tile_rows = tiles.shape[-1]
    width = weights.shape[-1]
    mats = weights.shape[0]
    table = history.reshape(-1, tile_rows, width)

    tiles_held = table.shape[0]
    table = table.reshape(tiles_held, CHUNKS, tile_rows // CHUNKS, width)
    levels = rooms(planes, blk_offset.shape[1])
    words = requests(planes, levels, tiles_held, blk_owner.reshape(1, -1), blk_offset)
    first, codes, top = ask(planes, reps, table, words)
    pulled = lax.switch(
        top[0, 0],
        [
            functools.partial(pull, planes, level, far_room, near_room)
            for level, (far_room, near_room) in enumerate(levels)
        ],
        table, first, codes,
    )
    fresh, grad_x, grad_w = layer(
        planes, reps, blk_relation, pulled, tiles, features[0], cotangent[0], weights
    )
    fresh, grad_x, grad_w = hand_over(fresh, grad_x, grad_w)
    return fresh[None], grad_x[None], grad_w


def solution(mesh):
    planes = mesh.shape["hist"] // PLANE
    in_specs = (
        P("rep", "hist", None),
        P("rep", "hist", None),
        P("rep", "hist", None),
        P("rep", "hist"),
        P("rep", "hist"),
        P("rep", "hist", None, None),
        P(),
        P("rep", "hist", None),
    )
    out_specs = (P("rep", "hist", None), P("rep", "hist", None), P(None, "hist"))
    return jax.shard_map(
        functools.partial(on_device, planes, mesh.shape["rep"]),
        mesh=mesh, in_specs=in_specs, out_specs=out_specs, check_vma=False,
    )
```
